32 devices in a mesh: groups: 2 (over y), tile: 16 (over z, x, core).
Axes of the slice: x: 2, y: 2, z: 4, core: 2. Of those that a mesh axis runs over, the one named last changes fastest.
Arguments:
- features: bfloat16 [192, 16, 16, 256], P(('groups', 'tile')), parts along dimension 0, may hold values from -6 to 6
- weights: bfloat16 [9, 256, 256], replicated, may hold values from -0.125 to 0.125
- grad_out: bfloat16 [192, 16, 16, 256], P(('groups', 'tile')), parts along dimension 0, may hold values from -6 to 6
- tile_pos: int32 [192], P(('groups', 'tile')), parts along dimension 0, may hold values from -1 to 7, as said below
- neighbours: int32 [192, 8], P(('groups', 'tile')), parts along dimension 0, may hold values from -1 to 15, as said below
Outputs:
- activation: bfloat16 [192, 16, 16, 256], P(('groups', 'tile')), parts along dimension 0
- weight_grad: float32 [18, 256, 256], P('groups'), parts along dimension 0
- input_grad: bfloat16 [192, 16, 16, 256], P(('groups', 'tile')), parts along dimension 0
The draws below stay inside these ranges and needn't reach their ends.
There are 2 independent parts, one for each index of `groups`. The reference program is written for one: setup_inputs(seed, part) draws one part's arguments, and reference() takes and returns one part's arrays. A program takes and returns all parts, laid end to end along the dimension named above; an argument that names none is the same for every part. Nothing has to cross between parts.
Inputs may be any that keep to these rules, and one draw needn't show every extreme that they name: `tile_pos`: each device's 6 slots hold the tissue tiles of its band of 2 x 4 tiles first, in raster order, then empty slots; every device holds 2 or more tissue tiles and at least one device holds 6. A code c names slot c % 6 of the device whose index is the own index plus c // 6 - 1; codes of left and right neighbours name the own device, up and up-diagonal neighbours lie on the own or the preceding device, down and down-diagonal ones on the own or the following device. Neighbours are tissue tiles of the slide's grid and the relation is symmetric; empty slots and missing neighbours have -1.
All inputs are finite; a program needn't handle non-finite values.
Results may differ from the reference program's by a relative error of at most 0.0049.
Values may be sent and summed in bfloat16 or wider, within the bound.
No kernel may reach another device: no remote copies, remote signals or barrier semaphores. Data moves between devices by JAX's collectives and lax.ppermute only.
A program may use at most 64 MiB of HBM per device.

```python
import math
import jax
import jax.numpy as jnp
from jax import lax

CH = 256
SIDE = 16
TILE_DEV = 6
BAND = 2
GRID_COLS = 4
TILES = 96


ROW_STEPS = (-1, 1, 0, 0, -1, -1, 1, 1)


COL_STEPS = (0, 0, -1, 1, -1, 1, -1, 1)


def slide_layout(key):
    key = jax.random.fold_in(key, 7)
    band_count = TILES // TILE_DEV
    cell_count = BAND * GRID_COLS
    spread = TILE_DEV - 2
    key_first, key_second, key_full, key_order = jax.random.split(key, 4)
    first_draw = jax.random.randint(key_first, (band_count,), 0, spread + 1)
    second = jax.random.randint(key_second, (band_count,), 0, spread + 1)
    counts = 2 + first_draw * second // spread
    chosen = jax.random.randint(key_full, (), 1, band_count)
    band_ids = jnp.arange(band_count, dtype=jnp.int32)
    counts = jnp.where(band_ids == chosen, TILE_DEV, counts).astype(jnp.int32)
    cell_ids = jnp.arange(cell_count, dtype=jnp.int32)
    ranking = jax.vmap(lambda single: jax.random.permutation(single, cell_count))(jax.random.split(key_order, band_count)).astype(jnp.int32)
    ranking = jnp.where(band_ids[:, None] == chosen, cell_ids[None, :], ranking)
    last_rank = ranking[:, cell_count - 1:cell_count]
    bumped = jnp.where(cell_ids[None, :] == cell_count - 1, 0, jnp.where(ranking < last_rank, ranking + 1, ranking))
    ranking = jnp.where(band_ids[:, None] == chosen - 1, bumped, ranking)
    tissue = ranking < counts[:, None]
    raster_order = jnp.argsort(jnp.where(tissue, 0, cell_count) + cell_ids[None, :], axis=1).astype(jnp.int32)
    slot_ids = jnp.arange(TILE_DEV, dtype=jnp.int32)
    positions = jnp.where(slot_ids[None, :] < counts[:, None], raster_order[:, :TILE_DEV], -1).astype(jnp.int32)
    slot_of = jnp.where(tissue, jnp.cumsum(tissue.astype(jnp.int32), axis=1) - 1, -1)
    tile_rows = positions // GRID_COLS
    tile_cols = positions % GRID_COLS
    row_steps = jnp.array(ROW_STEPS, dtype=jnp.int32)
    col_steps = jnp.array(COL_STEPS, dtype=jnp.int32)
    target_row = tile_rows[:, :, None] + row_steps[None, None, :]
    target_col = tile_cols[:, :, None] + col_steps[None, None, :]
    band_step = jnp.where(target_row < 0, -1, jnp.where(target_row >= BAND, 1, 0))
    target_band = band_ids[:, None, None] + band_step
    inside = (positions[:, :, None] >= 0) & (target_col >= 0) & (target_col < GRID_COLS)
    inside = inside & (target_band >= 0) & (target_band < band_count)
    target_cell = jnp.clip((target_row - band_step * BAND) * GRID_COLS + target_col, 0, cell_count - 1)
    found_slot = slot_of[jnp.clip(target_band, 0, band_count - 1), target_cell]
    inside = inside & (found_slot >= 0)
    link_codes = jnp.where(inside, (band_step + 1) * TILE_DEV + found_slot, -1).astype(jnp.int32)
    return (positions.reshape(TILES), link_codes.reshape(TILES, 8))


def draw_tile_pos(key, part):
    return slide_layout(key)[0]


def draw_neighbours(key, part):
    return slide_layout(key)[1]


def levels(stream_key, dims, cuts, least, top_value):
    factor_of, own = 1.0, jax.random.fold_in(stream_key, 6)
    for position, shards_of in cuts:
        steps = jnp.exp(jax.random.uniform(jax.random.fold_in(own, position), (shards_of,), jnp.float32, least / len(cuts), top_value / len(cuts)))
        factor_of = factor_of * jnp.repeat(steps, dims[position] // shards_of).reshape([-1 if axis == position else 1 for axis in range(len(dims))])
    return factor_of


def bell_draw(key, extent, width, reach, shards=(), kind=jnp.bfloat16):
    drawn = width * jax.random.normal(key, extent, jnp.float32)
    if shards:
        drawn = drawn * levels(key, extent, shards, -0.22, 0.18)
    return jnp.clip(drawn, -reach, reach).astype(kind)


def setup_inputs(seed: int = 0, part: int = 0) -> dict:
    key_list = jax.random.split(jax.random.key(seed), 6)
    part_splits = jax.random.split(jax.random.fold_in(key_list[5], part), 6)
    features = bell_draw(part_splits[0], (TILES, SIDE, SIDE, CH), 1.0, 6.0, ((0, 16),))
    weights = bell_draw(key_list[1], (9, CH, CH), (9 * CH) ** -0.5, 0.125)
    grad_out = bell_draw(part_splits[2], (TILES, SIDE, SIDE, CH), 1.0, 6.0, ((0, 16),))
    tile_pos = draw_tile_pos(jax.random.fold_in(jax.random.fold_in(key_list[5], part), 71), part)
    neighbours = draw_neighbours(jax.random.fold_in(jax.random.fold_in(key_list[5], part), 71), part)
    return dict(features=features, weights=weights, grad_out=grad_out, tile_pos=tile_pos, neighbours=neighbours)


EDGE_PICK = (1, 0, 3, 2, 1, 1, 0, 0)
ROOT_HALF = 0.7071067811865476
INV_ROOT_TAU = 0.3989422804014327

def gelu_value(preact):
    return preact * (0.5 * (1.0 + lax.erf(preact * ROOT_HALF)))

def gelu_slope(preact):
    cumulative = 0.5 * (1.0 + lax.erf(preact * ROOT_HALF))
    density = jnp.exp(-0.5 * preact * preact) * INV_ROOT_TAU
    return cumulative + preact * density

def edge_rims(field_map):
    return jnp.stack([field_map[:, 0], field_map[:, -1], field_map[:, :, 0], field_map[:, :, -1]], axis=1)

def surround(center, gathered):
    upper_row = jnp.concatenate([gathered[:, 4, -1:], gathered[:, 0], gathered[:, 5, :1]], axis=1)
    lower_row = jnp.concatenate([gathered[:, 6, -1:], gathered[:, 1], gathered[:, 7, :1]], axis=1)
    middle = jnp.concatenate([gathered[:, 2][:, :, None], center, gathered[:, 3][:, :, None]], axis=2)
    return jnp.concatenate([upper_row[:, None], middle, lower_row[:, None]], axis=1)

def tap_matrix(extended, flipped):
    side_cells = extended.shape[1] - 2
    pieces = []
    for row_tap in range(3):
        for col_tap in range(3):
            row_start = 2 - row_tap if flipped else row_tap
            col_start = 2 - col_tap if flipped else col_tap
            pieces.append(extended[:, row_start:row_start + side_cells, col_start:col_start + side_cells])
    stacked = jnp.concatenate(pieces, axis=-1)
    return stacked.reshape(-1, stacked.shape[-1])

def band_extend(center, edge_table, link_rows, band_index):
    tile_dev = center.shape[0]
    edge_picks = jnp.array(EDGE_PICK, dtype=jnp.int32)
    linked = link_rows >= 0
    source = (band_index * tile_dev + link_rows - tile_dev) * 4 + edge_picks[None, :]
    clipped = jnp.clip(jnp.where(linked, source, 0), 0, edge_table.shape[0] - 1).astype(jnp.int32)
    gathered = jnp.take(edge_table, clipped.reshape(-1), axis=0).reshape(linked.shape + edge_table.shape[1:])
    gathered = jnp.where(linked[:, :, None, None], gathered, jnp.zeros((), gathered.dtype))
    return surround(center, gathered)

def reference(features, weights, grad_out, tile_pos, neighbours):
    band_count = TILES // TILE_DEV
    tissue = (tile_pos >= 0).astype(jnp.float32)
    weight_mat = weights.reshape(9 * CH, CH)
    flip_mat = jnp.transpose(weights, (0, 2, 1)).reshape(9 * CH, CH)
    table_x = edge_rims(features).reshape(TILES * 4, SIDE, CH)
    band_ids = jnp.arange(band_count, dtype=jnp.int32)

    def forward(band_index):
        first_slot = band_index * TILE_DEV
        center = lax.dynamic_slice_in_dim(features, first_slot, TILE_DEV, 0)
        link_rows = lax.dynamic_slice_in_dim(neighbours, first_slot, TILE_DEV, 0)
        tissue_gate = lax.dynamic_slice_in_dim(tissue, first_slot, TILE_DEV, 0)
        grad_tiles = lax.dynamic_slice_in_dim(grad_out, first_slot, TILE_DEV, 0)
        extended = band_extend(center, table_x, link_rows, band_index)
        preact = jnp.dot(tap_matrix(extended, False), weight_mat, preferred_element_type=jnp.float32)
        preact = preact.reshape(TILE_DEV, SIDE, SIDE, CH)
        gate_cells = tissue_gate[:, None, None, None]
        act_map = (gelu_value(preact) * gate_cells).astype(jnp.bfloat16)
        slope_map = (grad_tiles.astype(jnp.float32) * gelu_slope(preact) * gate_cells).astype(jnp.bfloat16)
        return (act_map, slope_map)
    activation, pre_grad = lax.map(forward, band_ids)
    activation = activation.reshape(TILES, SIDE, SIDE, CH)
    pre_grad = pre_grad.reshape(TILES, SIDE, SIDE, CH)
    table_g = edge_rims(pre_grad).reshape(TILES * 4, SIDE, CH)

    def backward(running, band_index):
        first_slot = band_index * TILE_DEV
        center_x = lax.dynamic_slice_in_dim(features, first_slot, TILE_DEV, 0)
        center_g = lax.dynamic_slice_in_dim(pre_grad, first_slot, TILE_DEV, 0)
        link_rows = lax.dynamic_slice_in_dim(neighbours, first_slot, TILE_DEV, 0)
        tissue_gate = lax.dynamic_slice_in_dim(tissue, first_slot, TILE_DEV, 0)
        ext_x = band_extend(center_x, table_x, link_rows, band_index)
        ext_g = band_extend(center_g, table_g, link_rows, band_index)
        running = running + lax.dot_general(tap_matrix(ext_x, False), center_g.reshape(-1, CH), (((0,), (0,)), ((), ())), preferred_element_type=jnp.float32)
        back_map = jnp.dot(tap_matrix(ext_g, True), flip_mat, preferred_element_type=jnp.float32)
        back_map = back_map.reshape(TILE_DEV, SIDE, SIDE, CH) * tissue_gate[:, None, None, None]
        return (running, back_map.astype(jnp.bfloat16))
    summed, input_grad = lax.scan(backward, jnp.zeros((9 * CH, CH), jnp.float32), band_ids)
    grad_scale = 1.0 / math.sqrt(TILES * SIDE * SIDE)
    weight_grad = (summed * grad_scale).reshape(9, CH, CH)
    return (activation, weight_grad, input_grad.reshape(TILES, SIDE, SIDE, CH))
```

```python
import math

import jax
import jax.numpy as jnp
from jax import lax
from jax.sharding import PartitionSpec as P

EDGE_PICK = (1, 0, 3, 2, 1, 1, 0, 0)
ROOT_HALF = 0.7071067811865476
INV_ROOT_TAU = 0.3989422804014327


def from_behind(value, axis, steps):
    count = lax.axis_size(axis)
    initial, last = (max(0, -steps), min(count, count - steps))
    return lax.ppermute(value, axis, [(source, source + steps) for source in range(initial, last)])


def gelu_value(preact):
    return preact * (0.5 * (1.0 + lax.erf(preact * ROOT_HALF)))


def gelu_slope(preact):
    cumulative = 0.5 * (1.0 + lax.erf(preact * ROOT_HALF))
    density = jnp.exp(-0.5 * preact * preact) * INV_ROOT_TAU
    return cumulative + preact * density


def edge_rims(field_map):
    return jnp.stack(
        [field_map[:, 0], field_map[:, -1], field_map[:, :, 0], field_map[:, :, -1]], axis=1
    )


def surround(center, gathered):
    upper_row = jnp.concatenate([gathered[:, 4, -1:], gathered[:, 0], gathered[:, 5, :1]], axis=1)
    lower_row = jnp.concatenate([gathered[:, 6, -1:], gathered[:, 1], gathered[:, 7, :1]], axis=1)
    middle = jnp.concatenate(
        [gathered[:, 2][:, :, None], center, gathered[:, 3][:, :, None]], axis=2
    )
    return jnp.concatenate([upper_row[:, None], middle, lower_row[:, None]], axis=1)


def tap_matrix(extended, flipped):
    side_cells = extended.shape[1] - 2
    pieces = []
    for row_tap in range(3):
        for col_tap in range(3):
            row_start = 2 - row_tap if flipped else row_tap
            col_start = 2 - col_tap if flipped else col_tap
            pieces.append(
                extended[:, row_start : row_start + side_cells, col_start : col_start + side_cells]
            )
    stacked = jnp.concatenate(pieces, axis=-1)
    return stacked.reshape(-1, stacked.shape[-1])


def lookup(edge_table, source, linked):
    clipped = jnp.clip(jnp.where(linked, source, 0), 0, edge_table.shape[0] - 1)
    picked = jnp.take(edge_table, clipped.reshape(-1), axis=0).reshape(
        linked.shape + edge_table.shape[1:]
    )
    return jnp.where(linked[:, :, None, None], picked, jnp.zeros((), picked.dtype))


def narrow_sources(neighbours, edge_picks, tile_dev):
    anchor = neighbours // tile_dev
    own_slot = (neighbours - tile_dev) * 4 + edge_picks[None, :]
    return jnp.where(
        anchor == 1,
        own_slot,
        jnp.where(anchor == 0, 4 * tile_dev + neighbours, 3 * tile_dev + neighbours),
    )


def narrow_table(own_rims, upper_rows, lower_rows):
    tile_dev = own_rims.shape[0]
    side_cells = own_rims.shape[2]
    channels = own_rims.shape[3]
    return jnp.concatenate(
        [own_rims.reshape(4 * tile_dev, side_cells, channels), upper_rows, lower_rows], axis=0
    )


def forward_tiles(extended, grad_tiles, tissue_gate, weight_mat):
    tile_count = extended.shape[0]
    side_cells = extended.shape[1] - 2
    channels = weight_mat.shape[1]
    preact = jnp.dot(tap_matrix(extended, False), weight_mat, preferred_element_type=jnp.float32)
    preact = preact.reshape(tile_count, side_cells, side_cells, channels)
    gate_cells = tissue_gate[:, None, None, None]
    act_map = (gelu_value(preact) * gate_cells).astype(jnp.bfloat16)
    slope_map = (grad_tiles.astype(jnp.float32) * gelu_slope(preact) * gate_cells).astype(
        jnp.bfloat16
    )
    return (act_map, slope_map)


def weight_terms(ext_x, slope_map):
    return lax.dot_general(
        tap_matrix(ext_x, False),
        slope_map.reshape(-1, slope_map.shape[-1]),
        (((0,), (0,)), ((), ())),
        preferred_element_type=jnp.float32,
    )


def backward_tiles(ext_g, tissue_gate, flip_mat):
    tile_count = ext_g.shape[0]
    side_cells = ext_g.shape[1] - 2
    channels = flip_mat.shape[1]
    back_map = jnp.dot(tap_matrix(ext_g, True), flip_mat, preferred_element_type=jnp.float32)
    back_map = (
        back_map.reshape(tile_count, side_cells, side_cells, channels)
        * tissue_gate[:, None, None, None]
    )
    return back_map.astype(jnp.bfloat16)


def swap(value, bit):
    count = lax.axis_size("tile")
    return lax.ppermute(value, "tile", [(s, s ^ bit) for s in range(count)])


def scatter_step(total, bit):
    half = total.shape[0] // 2
    upper = (lax.axis_index("tile") & bit) != 0
    send = jnp.where(upper, total[:half], total[half:]).astype(jnp.bfloat16)
    keep = jnp.where(upper, total[half:], total[:half])
    return keep, send


def gather_step(own, other, bit):
    upper = (lax.axis_index("tile") & bit) != 0
    return jnp.concatenate([jnp.where(upper, other, own), jnp.where(upper, own, other)], axis=0)


def reduce_streams(streams, bits):
    pairs = [scatter_step(total, bit) for total, bit in zip(streams, bits)]
    got = [swap(send, bit) for (keep, send), bit in zip(pairs, bits)]
    return [keep + recv.astype(jnp.float32) for (keep, _), recv in zip(pairs, got)]


def gather_streams(streams, bits):
    got = [swap(own, bit) for own, bit in zip(streams, bits)]
    return [gather_step(own, other, bit) for own, other, bit in zip(streams, got, bits)]


def sum_over_tile(part):
    count = lax.axis_size("tile")
    if count < 16 or count & (count - 1):
        return lax.psum(part, "tile")
    (half,) = reduce_streams([part], [1])
    rows = half.shape[0] // 2
    orders = ((2, 4), (4, 2))
    streams = [half[:rows], half[rows:]]
    for level in range(2):
        streams = reduce_streams(streams, [order[level] for order in orders])
    piece = streams[0].shape[0]
    joined = jnp.concatenate(streams, axis=0)
    high = [8 << k for k in range(count.bit_length() - 4)]
    for bit in high[:-1]:
        (joined,) = reduce_streams([joined], [bit])
    mine = joined.astype(jnp.bfloat16)
    other = swap(mine, high[-1])
    joined = (mine.astype(jnp.float32) + other.astype(jnp.float32)).astype(jnp.bfloat16)
    for bit in reversed(high[:-1]):
        (joined,) = gather_streams([joined], [bit])
    streams = [joined[:piece], joined[piece:]]
    for level in (1, 0):
        streams = gather_streams(streams, [order[level] for order in orders])
    (whole,) = gather_streams([jnp.concatenate(streams, axis=0)], [1])
    return whole.astype(jnp.float32)


def body(features, weights, grad_out, tile_pos, neighbours):
    tile_dev = features.shape[0]
    side_cells = features.shape[1]
    channels = features.shape[3]
    devices = lax.axis_size("tile")
    tissue = (tile_pos >= 0).astype(jnp.float32)
    weight_mat = weights.reshape(9 * channels, channels)
    flip_mat = jnp.transpose(weights, (0, 2, 1)).reshape(9 * channels, channels)
    edge_picks = jnp.array(EDGE_PICK, dtype=jnp.int32)
    linked = neighbours >= 0
    rims_x = edge_rims(features)
    from_above = from_behind(rims_x[:, 1], "tile", 1)
    from_below = from_behind(rims_x[:, 0], "tile", -1)
    table_x = narrow_table(rims_x, from_above, from_below)
    source = narrow_sources(neighbours, edge_picks, tile_dev)
    ext_x = surround(features, lookup(table_x, source, linked))
    activation, pre_grad = forward_tiles(ext_x, grad_out, tissue, weight_mat)
    rims_g = edge_rims(pre_grad)
    grad_above = from_behind(rims_g[:, 1], "tile", 1)
    grad_below = from_behind(rims_g[:, 0], "tile", -1)
    table_g = narrow_table(rims_g, grad_above, grad_below)
    ext_g = surround(pre_grad, lookup(table_g, source, linked))
    weight_part = weight_terms(ext_x, pre_grad)
    grad_scale = 1.0 / math.sqrt(tile_dev * devices * side_cells * side_cells)
    summed = sum_over_tile(weight_part)
    weight_grad = (summed * grad_scale).reshape(9, channels, channels)
    input_grad = backward_tiles(ext_g, tissue, flip_mat)
    return (activation, weight_grad, input_grad)


def solution(mesh):
    in_specs = (
        P(("groups", "tile"), None, None, None),
        P(),
        P(("groups", "tile"), None, None, None),
        P(("groups", "tile")),
        P(("groups", "tile"), None),
    )
    out_specs = (
        P(("groups", "tile"), None, None, None),
        P("groups", None, None),
        P(("groups", "tile"), None, None, None),
    )
    return jax.shard_map(body, mesh=mesh, in_specs=in_specs, out_specs=out_specs, check_vma=False)
```

```python
import functools
import math

import jax
import jax.numpy as jnp
from jax import lax
from jax.experimental import pallas as pl
from jax.experimental.pallas import tpu as pltpu
from jax.sharding import PartitionSpec as P

ROOT_HALF = 0.7071067811865476
INV_ROOT_TAU = 0.3989422804014327
F32 = jnp.float32
BF16 = jnp.bfloat16
VMEM = pl.BlockSpec(memory_space=pltpu.VMEM)
SMEM = pl.BlockSpec(memory_space=pltpu.SMEM)
ANY = pl.BlockSpec(memory_space=pl.ANY)
LIMIT = 40 << 20


def shape_of(shape, dtype):
    return jax.ShapeDtypeStruct(shape, dtype)


def call(kernel, name, flops, moved, **options):
    return pl.pallas_call(
        kernel,
        name=name,
        compiler_params=pltpu.CompilerParams(vmem_limit_bytes=LIMIT),
        cost_estimate=pl.CostEstimate(flops=flops, bytes_accessed=moved, transcendentals=0),
        **options,
    )


def rows_from(own_rows, far_rows, code, first):
    slots = own_rows.shape[0]
    own = own_rows[jnp.clip(code - slots, 0, slots - 1)].astype(F32)
    far = far_rows[jnp.clip(code - first, 0, slots - 1)].astype(F32)
    inside = (code >= slots) & (code < 2 * slots)
    return jnp.where(inside, own, jnp.where(code >= 0, far, 0.0))


def put_columns(out, at, center, left, right):
    axis = center.ndim - 2
    side, channels = center.shape[-2:]
    cell = lax.broadcasted_iota(jnp.int32, center.shape, axis)
    shifted = pltpu.roll(jnp.where(cell == side - 1, left, center), 1, axis)
    out[at + (Ellipsis, slice(0, channels))] = shifted.astype(BF16)
    out[at + (Ellipsis, slice(channels, 2 * channels))] = center.astype(BF16)
    shifted = pltpu.roll(jnp.where(cell == 0, right, center), side - 1, axis)
    out[at + (Ellipsis, slice(2 * channels, 3 * channels))] = shifted.astype(BF16)


def put_inner(out, maps, codes, tile, at):
    slots = maps.shape[0]

    def neighbour(code):
        return jnp.where(code >= 0, maps[jnp.clip(code - slots, 0, slots - 1)].astype(F32), 0.0)

    put_columns(
        out, (at,), maps[tile].astype(F32), neighbour(codes[tile, 2]), neighbour(codes[tile, 3])
    )


def put_edges(out, first, last, up, down, codes, tile, at):
    slots = first.shape[0]
    top = [rows_from(last, up, codes[tile, j], 0) for j in (0, 4, 5)]
    put_columns(out, (at, 0), *top)
    bottom = [rows_from(first, down, codes[tile, j], 2 * slots) for j in (1, 6, 7)]
    put_columns(out, (at, 1), *bottom)


def rows_for(inner, edge, tile, step):
    side = inner.shape[1]
    if step == 1:
        return inner[tile]
    if step == 0:
        return jnp.concatenate([edge[tile, 0][None], inner[tile, : side - 1]], axis=0)
    return jnp.concatenate([inner[tile, 1:], edge[tile, 1][None]], axis=0)


def load_kernel(codes, maps, weights, grads, inner, weights_out, grads_out, held, sems):
    loads = [
        pltpu.make_async_copy(source, target, sems.at[k])
        for k, (source, target) in enumerate(
            [(maps, held), (weights, weights_out), (grads, grads_out)]
        )
    ]
    for load in loads:
        load.start()
    loads[0].wait()
    for tile in range(maps.shape[0]):
        put_inner(inner, held, codes, tile, tile)
    loads[1].wait()
    loads[2].wait()


def load(codes, maps, weights, grads):
    slots, side, _, channels = maps.shape
    return call(
        load_kernel,
        "load",
        1 << 20,
        6 << 20,
        in_specs=[SMEM, ANY, ANY, ANY],
        out_specs=[VMEM] * 3,
        out_shape=[
            shape_of((slots, side, side, 3 * channels), BF16),
            shape_of(weights.shape, BF16),
            shape_of(grads.shape, BF16),
        ],
        scratch_shapes=[pltpu.VMEM(maps.shape, BF16), pltpu.SemaphoreType.DMA((3,))],
    )(codes, maps, weights, grads)


def forward_kernel(
    codes, pos, inner, first, last, up, down, weights, grads,
    act, grad, edge, grad_first, grad_last, codes_held, pos_held, sems,
):
    slots, side, _, wide = inner.shape
    channels = wide // 3
    loads = [
        pltpu.make_async_copy(codes, codes_held, sems.at[0]),
        pltpu.make_async_copy(pos, pos_held, sems.at[1]),
    ]
    for item in loads:
        item.start()

    def product(tile, step):
        rows = rows_for(inner, edge, tile, step).reshape(side * side, wide)
        return jnp.dot(
            rows,
            weights[3 * step * channels : 3 * (step + 1) * channels],
            preferred_element_type=F32,
        )

    for item in loads:
        item.wait()
    for tile in range(slots):
        put_edges(edge, first, last, up, down, codes_held, tile, tile)
    for tile in range(slots):
        value = product(tile, 1) + product(tile, 0) + product(tile, 2)
        gate = jnp.where(pos_held[tile] >= 0, 1.0, 0.0)
        cumulative = 0.5 * (1.0 + lax.erf(value * ROOT_HALF))
        density = jnp.exp(-0.5 * value * value) * INV_ROOT_TAU
        cells = (side, side, channels)
        act[tile] = (value * cumulative * gate).astype(BF16).reshape(cells)
        slope = cumulative + value * density
        outer = grads[tile].astype(F32).reshape(side * side, channels)
        made = (outer * slope * gate).astype(BF16).reshape(cells)
        grad[tile] = made
        grad_first[tile] = made[0]
        grad_last[tile] = made[side - 1]


def forward(codes, pos, inner, first, last, up, down, weights, grads):
    slots, side, _, wide = inner.shape
    cells = grads.shape
    return call(
        forward_kernel,
        "forward",
        2 * slots * side * side * wide * wide,
        8 << 20,
        in_specs=[ANY, ANY] + [VMEM] * 7,
        out_specs=[VMEM] * 5,
        out_shape=[
            shape_of(cells, BF16),
            shape_of(cells, BF16),
            shape_of((slots, 2, side, wide), BF16),
            shape_of(first.shape, BF16),
            shape_of(first.shape, BF16),
        ],
        scratch_shapes=[
            pltpu.SMEM(codes.shape, jnp.int32),
            pltpu.SMEM(pos.shape, jnp.int32),
            pltpu.SemaphoreType.DMA((2,)),
        ],
    )(codes, pos, inner, first, last, up, down, weights, grads)


def kernel_grad_kernel(half, inner, edge, grad, out):
    slots, side, _, channels = grad.shape
    lanes = channels // 2
    outer = grad[...].reshape(slots * side * side, channels)
    for row_step in range(3):
        for col_step in range(3):
            start = pl.multiple_of(col_step * channels + half[0] * lanes, lanes)
            part = pl.ds(start, lanes)
            if row_step == 1:
                rows = inner[:, :, :, part]
            elif row_step == 0:
                rows = jnp.concatenate([edge[:, :1, :, part], inner[:, : side - 1, :, part]], axis=1)
            else:
                rows = jnp.concatenate([inner[:, 1:, :, part], edge[:, 1:, :, part]], axis=1)
            made = lax.dot_general(
                rows.reshape(slots * side * side, lanes),
                outer,
                (((0,), (0,)), ((), ())),
                preferred_element_type=F32,
            )
            out[:, 3 * row_step + col_step] = made.reshape(4, lanes // 4, channels).astype(out.dtype)


def kernel_grad(half, inner, edge, grad, dtype, name):
    slots, side, _, channels = grad.shape
    return call(
        kernel_grad_kernel,
        name,
        9 * slots * side * side * channels * channels,
        6 << 20,
        in_specs=[SMEM, VMEM, VMEM, VMEM],
        out_specs=VMEM,
        out_shape=shape_of((4, 9, channels // 8, channels), dtype),
    )(half, inner, edge, grad)


def spread_kernel(quad, keep, recv, own, *sends):
    own[...] = keep[quad[0]] + recv[quad[0]].astype(F32)
    for k, send in enumerate(sends):
        other = quad[0] ^ (k + 1)
        send[...] = (keep[other] + recv[other].astype(F32)).astype(BF16)


def spread(quad, keep, recv):
    piece = keep.shape[1:]
    return call(
        spread_kernel,
        "spread",
        1 << 20,
        3 << 20,
        in_specs=[SMEM, VMEM, VMEM],
        out_specs=[VMEM] * 4,
        out_shape=[shape_of(piece, F32)] + [shape_of(piece, BF16)] * 3,
    )(quad, keep, recv)


def collect_kernel(scale, place, *refs):
    out = refs[-1]
    pieces = refs[:-1]
    depth = pieces[0].shape[1]
    for k, piece in enumerate(pieces):
        half = place[0] if k < 4 else 1 - place[0]
        start = pl.multiple_of((half * 4 + (place[1] ^ (k % 4))) * depth, depth)
        out[:, pl.ds(start, depth), :] = piece[...].astype(F32) * scale


def collect(place, pieces, scale):
    taps, depth, channels = pieces[0].shape
    return call(
        functools.partial(collect_kernel, scale),
        "collect",
        1 << 20,
        4 << 20,
        in_specs=[SMEM] + [VMEM] * 8,
        out_specs=VMEM,
        out_shape=shape_of((taps, 8 * depth, channels), F32),
    )(place, *pieces)


def backward_kernel(tiles, codes, pos, grad, first, last, up, down, weights, out, inner, edge):
    slots, side, _, channels = grad.shape
    for k, tile in enumerate(tiles):
        put_inner(inner, grad, codes, tile, k)
        put_edges(edge, first, last, up, down, codes, tile, k)
    for k, tile in enumerate(tiles):
        total = None
        for row_step in range(3):
            rows = rows_for(inner, edge, k, row_step).reshape(side * side, 3 * channels)
            for col_step in range(3):
                tap = 3 * (2 - row_step) + 2 - col_step
                made = lax.dot_general(
                    rows[:, col_step * channels : (col_step + 1) * channels],
                    weights[tap * channels : (tap + 1) * channels],
                    (((1,), (1,)), ((), ())),
                    preferred_element_type=F32,
                )
                total = made if total is None else total + made
        gate = jnp.where(pos[tile] >= 0, 1.0, 0.0)
        out[k] = (total * gate).astype(BF16).reshape(side, side, channels)


def backward(tiles, codes, pos, grad, first, last, up, down, weights):
    slots, side, _, channels = grad.shape
    count = len(tiles)
    return call(
        functools.partial(backward_kernel, tiles),
        "backward",
        18 * count * side * side * channels * channels,
        4 << 20,
        in_specs=[SMEM, SMEM] + [VMEM] * 6,
        out_specs=VMEM,
        out_shape=shape_of((count, side, side, channels), BF16),
        scratch_shapes=[
            pltpu.VMEM((count, side, side, 3 * channels), BF16),
            pltpu.VMEM((count, 2, side, 3 * channels), BF16),
        ],
    )(codes, pos, grad, first, last, up, down, weights)


def from_behind(value, steps):
    count = lax.axis_size("tile")
    begin, end = max(0, -steps), min(count, count - steps)
    return lax.ppermute(value, "tile", [(source, source + steps) for source in range(begin, end)])


def swap(value, bit):
    count = lax.axis_size("tile")
    return lax.ppermute(value, "tile", [(source, source ^ bit) for source in range(count)])


def sum_piece(own, sends, high):
    for k, send in enumerate(sends):
        sends[k] = swap(send, 2 * (k + 1))
    total = own + sends[0].astype(F32) + sends[1].astype(F32) + sends[2].astype(F32)
    index = lax.axis_index("tile")
    for bit in high[:-1]:
        rows = total.shape[0] * total.shape[1] // 2
        flat = total.reshape(2, rows, total.shape[2])
        upper = (index & bit) != 0
        arrived = swap(jnp.where(upper, flat[0], flat[1]).astype(BF16), bit)
        total = (jnp.where(upper, flat[1], flat[0]) + arrived.astype(F32))[None]
    mine = total.astype(BF16)
    other = swap(mine, high[-1])
    total = (mine.astype(F32) + other.astype(F32)).astype(BF16)
    for bit in reversed(high[:-1]):
        upper = (index & bit) != 0
        other = swap(total, bit)
        total = jnp.concatenate(
            [jnp.where(upper, other, total), jnp.where(upper, total, other)], axis=1
        )
    return total.reshape(own.shape)


def body(features, weights, grad_out, tile_pos, neighbours):
    slots, side, _, channels = features.shape
    devices = lax.axis_size("tile")
    flat = weights.reshape(9 * channels, channels)
    first, last = features[:, 0], features[:, -1]
    above = from_behind(last, 1)
    below = from_behind(first, -1)
    inner, flat, grads = load(neighbours, features, flat, grad_out)
    activation, grad, edge, grad_first, grad_last = forward(
        neighbours, tile_pos, inner, first, last, above, below, flat, grads
    )
    index = lax.axis_index("tile").astype(jnp.int32)
    core = index & 1
    quad = (index >> 1) & 3
    send = kernel_grad((1 - core).reshape(1), inner, edge, grad, BF16, "kernel_grad_sent")
    recv = swap(send, 1)
    keep = kernel_grad(core.reshape(1), inner, edge, grad, F32, "kernel_grad_kept")
    own, *sends = spread(quad.reshape(1), keep, recv)
    high = [8 << k for k in range(devices.bit_length() - 4)]
    piece = sum_piece(own, sends, high)
    pieces = [piece] + [swap(piece, 2 * k) for k in (1, 2, 3)]
    pieces += [swap(item, 1) for item in pieces]
    scale = 1.0 / math.sqrt(slots * devices * side * side)
    weight_grad = collect(jnp.stack([core, quad]), pieces, scale)
    grad_above = from_behind(grad_last, 1)
    grad_below = from_behind(grad_first, -1)
    middle = slots // 2
    parts = [
        backward(
            tiles, neighbours, tile_pos, grad, grad_first, grad_last, grad_above, grad_below, flat
        )
        for tiles in (tuple(range(middle)), tuple(range(middle, slots)))
    ]
    return (activation, weight_grad, jnp.concatenate(parts, axis=0))


def solution(mesh):
    in_specs = (
        P(("groups", "tile"), None, None, None),
        P(),
        P(("groups", "tile"), None, None, None),
        P(("groups", "tile")),
        P(("groups", "tile"), None),
    )
    out_specs = (
        P(("groups", "tile"), None, None, None),
        P("groups", None, None),
        P(("groups", "tile"), None, None, None),
    )
    return jax.shard_map(body, mesh=mesh, in_specs=in_specs, out_specs=out_specs, check_vma=False)
```

```python
import functools
import math

import jax
import jax.numpy as jnp
from jax import lax
from jax.experimental import pallas as pl
from jax.experimental.pallas import tpu as pltpu
from jax.sharding import PartitionSpec as P


ROOT_HALF = 0.7071067811865476
INV_ROOT_TAU = 0.3989422804014327
F32 = jnp.float32
BF16 = jnp.bfloat16
VMEM = pl.BlockSpec(memory_space=pltpu.VMEM)
SMEM = pl.BlockSpec(memory_space=pltpu.SMEM)
ANY = pl.BlockSpec(memory_space=pl.ANY)
LIMIT = 16 << 20


def shape_of(shape, dtype):
    return jax.ShapeDtypeStruct(shape, dtype)


def held(shape, dtype):
    return pltpu.VMEM(shape, dtype)


def far(value):
    return pltpu.with_memory_space_constraint(value, pltpu.HBM)


def call(kernel, flops, moved, **options):
    return pl.pallas_call(
        kernel,
        compiler_params=pltpu.CompilerParams(vmem_limit_bytes=LIMIT),
        cost_estimate=pl.CostEstimate(flops=flops, bytes_accessed=moved, transcendentals=0),
        **options,
    )


def place():
    index = lax.axis_index("tile").astype(jnp.int32)
    core = lax.rem(index, 2)
    low, high = lax.rem(lax.div(index, 2), 2), lax.rem(lax.div(index, 4), 2)
    return core, jnp.where(core == 0, low, high), jnp.where(core == 0, high, low)


def rows_from(own_rows, far_rows, code, first):
    slots = own_rows.shape[0]
    own = own_rows[jnp.clip(code - slots, 0, slots - 1)].astype(F32)
    far = far_rows[jnp.clip(code - first, 0, slots - 1)].astype(F32)
    inside = (code >= slots) & (code < 2 * slots)
    return jnp.where(inside, own, jnp.where(code >= 0, far, 0.0))


def put_columns(out, at, center, left, right):
    axis = center.ndim - 2
    side, channels = center.shape[-2:]
    cell = lax.broadcasted_iota(jnp.int32, center.shape, axis)
    shifted = pltpu.roll(jnp.where(cell == side - 1, left, center), 1, axis)
    out[at + (Ellipsis, slice(0, channels))] = shifted.astype(BF16)
    out[at + (Ellipsis, slice(channels, 2 * channels))] = center.astype(BF16)
    shifted = pltpu.roll(jnp.where(cell == 0, right, center), side - 1, axis)
    out[at + (Ellipsis, slice(2 * channels, 3 * channels))] = shifted.astype(BF16)


def put_inner(out, maps, codes, tile, at):
    slots = maps.shape[0]

    def neighbour(code):
        return jnp.where(code >= 0, maps[jnp.clip(code - slots, 0, slots - 1)].astype(F32), 0.0)

    put_columns(
        out, (at,), maps[tile].astype(F32), neighbour(codes[tile, 2]), neighbour(codes[tile, 3])
    )


def put_edges(out, first, last, up, down, codes, tile, at):
    slots = first.shape[0]
    top = [rows_from(last, up, codes[tile, j], 0) for j in (0, 4, 5)]
    put_columns(out, (at, 0), *top)
    bottom = [rows_from(first, down, codes[tile, j], 2 * slots) for j in (1, 6, 7)]
    put_columns(out, (at, 1), *bottom)


def rows_for(inner, edge, tile, step):
    side = inner.shape[1]
    if step == 1:
        return inner[tile]
    if step == 0:
        return jnp.concatenate([edge[tile, 0][None], inner[tile, : side - 1]], axis=0)
    return jnp.concatenate([inner[tile, 1:], edge[tile, 1][None]], axis=0)


def load_kernel(codes, maps, weights, grads, inner, weights_out, grads_out, tiles, sems):
    loads = [
        pltpu.make_async_copy(source, target, sems.at[k])
        for k, (source, target) in enumerate(
            [(maps, tiles), (weights, weights_out), (grads, grads_out)]
        )
    ]
    for load in loads:
        load.start()
    loads[0].wait()
    for tile in range(maps.shape[0]):
        put_inner(inner, tiles, codes, tile, tile)
    loads[1].wait()
    loads[2].wait()


def load(codes, maps, weights, grads):
    slots, side, _, channels = maps.shape
    return call(
        load_kernel,
        1 << 20,
        6 << 20,
        in_specs=[SMEM, ANY, ANY, ANY],
        out_specs=[VMEM] * 3,
        out_shape=[
            held((slots, side, side, 3 * channels), BF16),
            held(weights.shape, BF16),
            held(grads.shape, BF16),
        ],
        scratch_shapes=[pltpu.VMEM(maps.shape, BF16), pltpu.SemaphoreType.DMA((3,))],
    )(far(codes), far(maps), far(weights), far(grads))


def forward_kernel(
    codes, pos, inner, first, last, up, down, weights, grads,
    act, grad, edge, grad_first, grad_last, codes_held, pos_held, sems,
):
    slots, side, _, wide = inner.shape
    channels = wide // 3
    loads = [
        pltpu.make_async_copy(codes, codes_held, sems.at[0]),
        pltpu.make_async_copy(pos, pos_held, sems.at[1]),
    ]
    for item in loads:
        item.start()

    def product(tile, step):
        rows = rows_for(inner, edge, tile, step).reshape(side * side, wide)
        return jnp.dot(
            rows,
            weights[3 * step * channels : 3 * (step + 1) * channels],
            preferred_element_type=F32,
        )

    for item in loads:
        item.wait()
    for tile in range(slots):
        put_edges(edge, first, last, up, down, codes_held, tile, tile)
    for tile in range(slots):
        value = product(tile, 1) + product(tile, 0) + product(tile, 2)
        gate = jnp.where(pos_held[tile] >= 0, 1.0, 0.0)
        cumulative = 0.5 * (1.0 + lax.erf(value * ROOT_HALF))
        density = jnp.exp(-0.5 * value * value) * INV_ROOT_TAU
        cells = (side, side, channels)
        act[tile] = (value * cumulative * gate).astype(BF16).reshape(cells)
        slope = cumulative + value * density
        outer = grads[tile].astype(F32).reshape(side * side, channels)
        made = (outer * slope * gate).astype(BF16).reshape(cells)
        grad[tile] = made
        grad_first[tile] = made[0]
        grad_last[tile] = made[side - 1]


def forward(codes, pos, inner, first, last, up, down, weights, grads):
    slots, side, _, wide = inner.shape
    cells = grads.shape
    return call(
        forward_kernel,
        2 * slots * side * side * wide * wide,
        8 << 20,
        in_specs=[ANY, ANY] + [VMEM] * 7,
        out_specs=[VMEM] * 5,
        out_shape=[
            shape_of(cells, BF16),
            held(cells, BF16),
            held((slots, 2, side, wide), BF16),
            held(first.shape, BF16),
            held(first.shape, BF16),
        ],
        scratch_shapes=[
            pltpu.SMEM(codes.shape, jnp.int32),
            pltpu.SMEM(pos.shape, jnp.int32),
            pltpu.SemaphoreType.DMA((2,)),
        ],
    )(far(codes), far(pos), inner, first, last, up, down, weights, grads)


def kernel_grad_kernel(other, inner, edge, grad, out):
    slots, side, _, channels = grad.shape
    lanes = channels // 2
    outer = grad[...].reshape(slots * side * side, channels)
    core = place()[0]
    half = 1 - core if other else core
    for row_step in range(3):
        for col_step in range(3):
            start = pl.multiple_of(col_step * channels + half * lanes, lanes)
            part = pl.ds(start, lanes)
            if row_step == 1:
                rows = inner[:, :, :, part]
            elif row_step == 0:
                rows = jnp.concatenate([edge[:, :1, :, part], inner[:, : side - 1, :, part]], axis=1)
            else:
                rows = jnp.concatenate([inner[:, 1:, :, part], edge[:, 1:, :, part]], axis=1)
            made = lax.dot_general(
                rows.reshape(slots * side * side, lanes),
                outer,
                (((0,), (0,)), ((), ())),
                preferred_element_type=F32,
            )
            out[:, 3 * row_step + col_step] = made.reshape(4, lanes // 4, channels).astype(out.dtype)


def kernel_grad(other, inner, edge, grad, dtype):
    slots, side, _, channels = grad.shape
    return call(
        functools.partial(kernel_grad_kernel, other),
        9 * slots * side * side * channels * channels,
        6 << 20,
        in_specs=[VMEM, VMEM, VMEM],
        out_specs=VMEM,
        out_shape=held((4, 9, channels // 8, channels), dtype),
    )(inner, edge, grad)


def spread_kernel(keep, recv, send):
    first_bit = place()[1]
    for k in range(2):
        piece = 2 * (1 - first_bit) + k
        send[k] = (keep[piece] + recv[piece].astype(F32)).astype(BF16)


def spread(keep, recv):
    return call(
        spread_kernel,
        1 << 20,
        2 << 20,
        in_specs=[VMEM, VMEM],
        out_specs=VMEM,
        out_shape=held((2,) + keep.shape[1:], BF16),
    )(keep, recv)


def narrow_kernel(flip, keep, recv, got, out):
    _, first_bit, second_bit = place()
    second = 1 - second_bit if flip else second_bit
    piece = 2 * first_bit + second
    total = keep[piece] + recv[piece].astype(F32) + got[second].astype(F32)
    out[...] = total.astype(out.dtype)


def narrow(flip, keep, recv, got, dtype):
    return call(
        functools.partial(narrow_kernel, flip),
        1 << 20,
        1 << 20,
        in_specs=[VMEM, VMEM, VMEM],
        out_specs=VMEM,
        out_shape=held(keep.shape[1:], dtype),
    )(keep, recv, got)


def collect_kernel(scale, plan, *refs):
    count = len(plan)
    core, first_bit, second_bit = place()
    own = core * 4 + 2 * first_bit + second_bit
    others = (1 - core) * 4 + 2 * second_bit + first_bit
    pieces, out = refs[:count], refs[-3]
    rows, sem = refs[-2], refs[-1]
    depth = pieces[0].shape[-2]
    copies = []
    for k, piece in enumerate(pieces):
        rows[k] = piece[...].astype(F32) * scale
        slot = (others if plan[k][0] else own) ^ plan[k][1]
        start = pl.multiple_of(slot * depth, depth)
        copy = pltpu.make_async_copy(rows.at[k], out.at[:, pl.ds(start, depth), :], sem.at[k])
        copy.start()
        copies.append(copy)
    for copy in copies:
        copy.wait()


def collect(plan, pieces, scale, whole, base):
    taps, depth, channels = pieces[0].shape
    count = len(pieces)
    operands = list(pieces)
    specs = [VMEM] * count
    aliases = {}
    if base is not None:
        operands.append(base)
        specs.append(ANY)
        aliases = {count: 0}
    return call(
        functools.partial(collect_kernel, scale, plan),
        1 << 20,
        count << 19,
        in_specs=specs,
        out_specs=ANY,
        out_shape=pltpu.HBM(whole, F32),
        input_output_aliases=aliases,
        scratch_shapes=[
            pltpu.VMEM((count, taps, depth, channels), F32),
            pltpu.SemaphoreType.DMA((count,)),
        ],
    )(*operands)


def backward_kernel(tiles, codes, pos, grad, first, last, up, down, weights, out, inner, edge):
    _, side, _, channels = grad.shape
    for k, tile in enumerate(tiles):
        put_inner(inner, grad, codes, tile, k)
        put_edges(edge, first, last, up, down, codes, tile, k)
    for k, tile in enumerate(tiles):
        total = None
        for row_step in range(3):
            rows = rows_for(inner, edge, k, row_step).reshape(side * side, 3 * channels)
            for col_step in range(3):
                tap = 3 * (2 - row_step) + 2 - col_step
                made = lax.dot_general(
                    rows[:, col_step * channels : (col_step + 1) * channels],
                    weights[tap * channels : (tap + 1) * channels],
                    (((1,), (1,)), ((), ())),
                    preferred_element_type=F32,
                )
                total = made if total is None else total + made
        gate = jnp.where(pos[tile] >= 0, 1.0, 0.0)
        out[k] = (total * gate).astype(BF16).reshape(side, side, channels)


def backward(tiles, codes, pos, grad, first, last, up, down, weights):
    _, side, _, channels = grad.shape
    count = len(tiles)
    return call(
        functools.partial(backward_kernel, tiles),
        18 * count * side * side * channels * channels,
        4 << 20,
        in_specs=[SMEM, SMEM] + [VMEM] * 6,
        out_specs=VMEM,
        out_shape=shape_of((count, side, side, channels), BF16),
        scratch_shapes=[
            pltpu.VMEM((count, side, side, 3 * channels), BF16),
            pltpu.VMEM((count, 2, side, 3 * channels), BF16),
        ],
    )(codes, pos, grad, first, last, up, down, weights)


def from_behind(value, steps):
    count = lax.axis_size("tile")
    begin, end = max(0, -steps), min(count, count - steps)
    return lax.ppermute(value, "tile", [(source, source + steps) for source in range(begin, end)])


def swap(value, bit):
    count = lax.axis_size("tile")
    return lax.ppermute(value, "tile", [(source, source ^ bit) for source in range(count)])


def crossed(value, even_bit, odd_bit):
    count = lax.axis_size("tile")
    pairs = [(s, s ^ (odd_bit if s & 1 else even_bit)) for s in range(count)]
    return lax.ppermute(value, "tile", pairs)


def sum_high(total, high):
    shape = total.shape
    index = lax.axis_index("tile")
    for bit in high[:-1]:
        flat = total.reshape(2, -1, shape[-1])
        upper = (index & bit) != 0
        arrived = swap(jnp.where(upper, flat[0], flat[1]).astype(BF16), bit)
        total = jnp.where(upper, flat[1], flat[0]) + arrived.astype(F32)
    mine = total.astype(BF16)
    other = swap(mine, high[-1])
    total = (mine.astype(F32) + other.astype(F32)).astype(BF16)
    for bit in reversed(high[:-1]):
        upper = (index & bit) != 0
        other = swap(total, bit)
        total = jnp.concatenate(
            [jnp.where(upper, other, total), jnp.where(upper, total, other)], axis=0
        )
    return total.reshape(shape)


def step(features, weights, grad_out, tile_pos, neighbours):
    slots, side, _, channels = features.shape
    devices = lax.axis_size("tile")
    flat = weights.reshape(9 * channels, channels)
    first, last = features[:, 0], features[:, -1]
    above = from_behind(last, 1)
    below = from_behind(first, -1)
    inner, flat, grads = load(neighbours, features, flat, grad_out)
    activation, grad, edge, grad_first, grad_last = forward(
        neighbours, tile_pos, inner, first, last, above, below, flat, grads
    )
    send = kernel_grad(True, inner, edge, grad, BF16)
    recv = swap(send, 1)
    keep = kernel_grad(False, inner, edge, grad, F32)
    sent = spread(keep, recv)
    got = crossed(sent, 2, 4)
    sent = narrow(True, keep, recv, got, BF16)
    got_next = crossed(sent, 4, 2)
    own = narrow(False, keep, recv, got, F32)
    piece = sum_high(
        own + got_next.astype(F32), [8 << k for k in range(devices.bit_length() - 4)]
    )
    scale = 1.0 / math.sqrt(slots * devices * side * side)
    whole = weights.shape
    near = crossed(piece, 4, 2)
    away = crossed(piece, 2, 4)
    its = swap(piece, 1)
    away_near = crossed(near, 2, 4)
    its_near = swap(near, 1)
    its_away = swap(away, 1)
    its_away_near = swap(away_near, 1)
    weight_grad = collect(
        ((0, 0), (0, 1), (1, 0), (1, 1), (0, 2)),
        [piece, near, its, its_near, away], scale, whole, None
    )
    weight_grad = collect(((0, 3), (1, 2)), [away_near, its_away], scale, whole, weight_grad)
    weight_grad = collect(((1, 3),), [its_away_near], scale, whole, weight_grad)
    grad_above = from_behind(grad_last, 1)
    grad_below = from_behind(grad_first, -1)
    input_grad = backward(
        tuple(range(slots)), neighbours, tile_pos, grad, grad_first, grad_last,
        grad_above, grad_below, weights.reshape(9 * channels, channels),
    )
    return (activation, weight_grad, input_grad)


def solution(mesh):
    in_specs = (
        P(("groups", "tile"), None, None, None),
        P(),
        P(("groups", "tile"), None, None, None),
        P(("groups", "tile")),
        P(("groups", "tile"), None),
    )
    out_specs = (
        P(("groups", "tile"), None, None, None),
        P("groups", None, None),
        P(("groups", "tile"), None, None, None),
    )
    return jax.shard_map(step, mesh=mesh, in_specs=in_specs, out_specs=out_specs, check_vma=False)
```

```python
import functools
import math

import jax
import jax.numpy as jnp
from jax import lax
from jax.experimental import pallas as pl
from jax.experimental.pallas import tpu as pltpu
from jax.sharding import PartitionSpec as P


ROOT_HALF = 0.7071067811865476
INV_ROOT_TAU = 0.3989422804014327
F32 = jnp.float32
BF16 = jnp.bfloat16
VMEM = pl.BlockSpec(memory_space=pltpu.VMEM)
SMEM = pl.BlockSpec(memory_space=pltpu.SMEM)
ANY = pl.BlockSpec(memory_space=pl.ANY)
LIMIT = 16 << 20


def held(shape, dtype):
    return pltpu.VMEM(shape, dtype)


def far(value):
    return pltpu.with_memory_space_constraint(value, pltpu.HBM)


def call(kernel, flops, moved, **options):
    return pl.pallas_call(
        kernel,
        compiler_params=pltpu.CompilerParams(vmem_limit_bytes=LIMIT),
        cost_estimate=pl.CostEstimate(flops=flops, bytes_accessed=moved, transcendentals=0),
        **options,
    )


def place():
    index = lax.axis_index("tile").astype(jnp.int32)
    return lax.rem(index, 2), lax.rem(lax.div(index, 2), 4)


def put_edges(out, own_row, side, slots, cross, link, codes, tile):
    core = place()[0]

    def named(code, row, begin, of_other_core):
        own = own_row(jnp.clip(code - slots, 0, slots - 1), row)
        away = jnp.clip(code - begin, 0, slots - 1)
        away = jnp.where(of_other_core, cross[away].astype(F32), link[away].astype(F32))
        inside = (code >= slots) & (code < 2 * slots)
        return jnp.where(inside, own, jnp.where(code >= 0, away, 0.0))

    top = [named(codes[tile, j], side - 1, 0, core == 1) for j in (0, 4, 5)]
    put_columns(out, (tile, 0), *top)
    bottom = [named(codes[tile, j], 0, 2 * slots, core == 0) for j in (1, 6, 7)]
    put_columns(out, (tile, 1), *bottom)


def put_sends(to_core, to_link, tile, first, last):
    even = place()[0] == 0
    to_core[tile] = jnp.where(even, last.astype(F32), first.astype(F32)).astype(BF16)
    to_link[tile] = jnp.where(even, first.astype(F32), last.astype(F32)).astype(BF16)


def put_columns(out, at, center, left, right):
    axis = center.ndim - 2
    side, channels = center.shape[-2:]
    cell = lax.broadcasted_iota(jnp.int32, center.shape, axis)
    shifted = pltpu.roll(jnp.where(cell == side - 1, left, center), 1, axis)
    out[at + (Ellipsis, slice(0, channels))] = shifted.astype(BF16)
    out[at + (Ellipsis, slice(channels, 2 * channels))] = center.astype(BF16)
    shifted = pltpu.roll(jnp.where(cell == 0, right, center), side - 1, axis)
    out[at + (Ellipsis, slice(2 * channels, 3 * channels))] = shifted.astype(BF16)


def put_inner(out, maps, codes, tile, at):
    slots = maps.shape[0]

    def neighbour(code):
        return jnp.where(code >= 0, maps[jnp.clip(code - slots, 0, slots - 1)].astype(F32), 0.0)

    put_columns(
        out, (at,), maps[tile].astype(F32), neighbour(codes[tile, 2]), neighbour(codes[tile, 3])
    )


def rows_for(inner, edge, tile, step):
    side = inner.shape[1]
    if step == 1:
        return inner[tile]
    if step == 0:
        return jnp.concatenate([edge[tile, 0][None], inner[tile, : side - 1]], axis=0)
    return jnp.concatenate([inner[tile, 1:], edge[tile, 1][None]], axis=0)


def inner_product(inner, weights, tile):
    side, _, wide = inner.shape[1:]
    channels = wide // 3
    total = jnp.dot(
        inner[tile].reshape(side * side, wide),
        weights[wide : 2 * wide],
        preferred_element_type=F32,
    )
    blank = jnp.zeros((side, channels), F32)
    short = (side - 1) * side
    upper = jnp.dot(
        inner[tile, : side - 1].reshape(short, wide), weights[:wide], preferred_element_type=F32
    )
    lower = jnp.dot(
        inner[tile, 1:].reshape(short, wide), weights[2 * wide :], preferred_element_type=F32
    )
    total += jnp.concatenate([blank, upper], axis=0)
    total += jnp.concatenate([lower, blank], axis=0)
    return total.reshape(side, side, channels)


def load_kernel(
    codes, maps, weights, grads, inner, weights_out, grads_out, to_core, to_link, tiles, sems
):
    loads = [
        pltpu.make_async_copy(source, target, sems.at[k])
        for k, (source, target) in enumerate(
            [(maps, tiles), (weights, weights_out), (grads, grads_out)]
        )
    ]
    for load in loads:
        load.start()
    loads[0].wait()
    slots, side = maps.shape[:2]
    for tile in range(slots):
        put_sends(to_core, to_link, tile, tiles[tile, 0], tiles[tile, side - 1])
        put_inner(inner, tiles, codes, tile, tile)
    loads[1].wait()
    loads[2].wait()


def load(codes, maps, weights, grads):
    slots, side, _, channels = maps.shape
    rims = (slots, side, channels)
    return call(
        load_kernel,
        1 << 20,
        6 << 20,
        in_specs=[SMEM, ANY, ANY, ANY],
        out_specs=[VMEM] * 5,
        out_shape=[
            held((slots, side, side, 3 * channels), BF16),
            held(weights.shape, BF16),
            held(grads.shape, BF16),
            held(rims, BF16),
            held(rims, BF16),
        ],
        scratch_shapes=[pltpu.VMEM(maps.shape, BF16), pltpu.SemaphoreType.DMA((3,))],
    )(far(codes), far(maps), far(weights), far(grads))


def product_kernel(inner, weights, partial):
    for tile in range(inner.shape[0]):
        partial[tile] = inner_product(inner, weights, tile)


def product(inner, weights):
    slots, side, _, wide = inner.shape
    return call(
        product_kernel,
        2 * slots * side * side * wide * wide,
        6 << 20,
        in_specs=[VMEM, VMEM],
        out_specs=VMEM,
        out_shape=held((slots, side, side, wide // 3), F32),
    )(inner, weights)


def forward_kernel(
    codes, pos, partial, inner, cross, link, weights, grads,
    act, grad, edge, to_core, to_link, codes_held, pos_held, sems,
):
    slots, side, _, channels = partial.shape
    wide = 3 * channels
    loads = [
        pltpu.make_async_copy(codes, codes_held, sems.at[0]),
        pltpu.make_async_copy(pos, pos_held, sems.at[1]),
    ]
    for item in loads:
        item.start()

    def finish(value, outer, gate):
        cumulative = 0.5 * (1.0 + lax.erf(value * ROOT_HALF))
        density = jnp.exp(-0.5 * value * value) * INV_ROOT_TAU
        slope = cumulative + value * density
        return (
            (value * cumulative * gate).astype(BF16),
            (outer.astype(F32) * slope * gate).astype(BF16),
        )

    loads[1].wait()
    gates = [jnp.where(pos_held[tile] >= 0, 1.0, 0.0) for tile in range(slots)]
    rows = slice(1, side - 1)
    for tile in range(slots):
        act[tile, rows], grad[tile, rows] = finish(
            partial[tile, rows], grads[tile, rows], gates[tile]
        )
    loads[0].wait()
    center = slice(channels, 2 * channels)
    for tile in range(slots):
        put_edges(
            edge, lambda slot, row: inner[slot, row, :, center].astype(F32),
            side, slots, cross, link, codes_held, tile,
        )
    for end, row, part in ((0, 0, 0), (1, side - 1, 2)):
        added = jnp.dot(
            edge[:, end].reshape(slots * side, wide),
            weights[part * wide : (part + 1) * wide],
            preferred_element_type=F32,
        ).reshape(slots, side, channels)
        for tile in range(slots):
            value, outer = finish(
                partial[tile, row] + added[tile], grads[tile, row], gates[tile]
            )
            act[tile, row] = value
            grad[tile, row] = outer
    for tile in range(slots):
        put_sends(to_core, to_link, tile, grad[tile, 0], grad[tile, side - 1])


def forward(codes, pos, partial, inner, cross, link, weights, grads):
    slots, side, _, channels = partial.shape
    wide = 3 * channels
    return call(
        forward_kernel,
        4 * slots * side * wide * channels,
        8 << 20,
        in_specs=[ANY, ANY] + [VMEM] * 6,
        out_specs=[VMEM] * 5,
        out_shape=[
            held(partial.shape, BF16),
            held(partial.shape, BF16),
            held((slots, 2, side, wide), BF16),
            held(cross.shape, BF16),
            held(cross.shape, BF16),
        ],
        scratch_shapes=[
            pltpu.SMEM(codes.shape, jnp.int32),
            pltpu.SMEM(pos.shape, jnp.int32),
            pltpu.SemaphoreType.DMA((2,)),
        ],
    )(far(codes), far(pos), partial, inner, cross, link, weights, grads)


def kernel_grad_kernel(other, inner, edge, grad, out):
    slots, side, _, channels = grad.shape
    lanes = channels // 2
    outer = grad[...].reshape(slots * side * side, channels)
    core = place()[0]
    half = 1 - core if other else core
    for row_step in range(3):
        for col_step in range(3):
            start = pl.multiple_of(col_step * channels + half * lanes, lanes)
            part = pl.ds(start, lanes)
            if row_step == 1:
                rows = inner[:, :, :, part]
            elif row_step == 0:
                rows = jnp.concatenate([edge[:, :1, :, part], inner[:, : side - 1, :, part]], axis=1)
            else:
                rows = jnp.concatenate([inner[:, 1:, :, part], edge[:, 1:, :, part]], axis=1)
            made = lax.dot_general(
                rows.reshape(slots * side * side, lanes),
                outer,
                (((0,), (0,)), ((), ())),
                preferred_element_type=F32,
            )
            out[:, 3 * row_step + col_step] = made.reshape(4, lanes // 4, channels).astype(out.dtype)


def kernel_grad(other, inner, edge, grad, dtype):
    slots, side, _, channels = grad.shape
    return call(
        functools.partial(kernel_grad_kernel, other),
        9 * slots * side * side * channels * channels,
        6 << 20,
        in_specs=[VMEM, VMEM, VMEM],
        out_specs=VMEM,
        out_shape=held((4, 9, channels // 8, channels), dtype),
    )(inner, edge, grad)


def spread_kernel(keep, recv, own, *sends):
    quad = place()[1]
    own[...] = keep[quad] + recv[quad].astype(F32)
    for k, send in enumerate(sends):
        other = quad ^ (k + 1)
        send[...] = (keep[other] + recv[other].astype(F32)).astype(BF16)


def spread(keep, recv):
    piece = keep.shape[1:]
    return call(
        spread_kernel,
        1 << 20,
        3 << 20,
        in_specs=[VMEM, VMEM],
        out_specs=[VMEM] * 4,
        out_shape=[held(piece, F32)] + [held(piece, BF16)] * 3,
    )(keep, recv)


def collect_kernel(scale, plan, *refs):
    count = len(plan)
    core, quad = place()
    pieces, out = refs[:count], refs[-3]
    rows, sem = refs[-2], refs[-1]
    depth = pieces[0].shape[-2]
    copies = []
    for k, piece in enumerate(pieces):
        rows[k] = piece[...].astype(F32) * scale
        half = 1 - core if plan[k][0] else core
        slot = half * 4 + (quad ^ plan[k][1])
        start = pl.multiple_of(slot * depth, depth)
        copy = pltpu.make_async_copy(rows.at[k], out.at[:, pl.ds(start, depth), :], sem.at[k])
        copy.start()
        copies.append(copy)
    for copy in copies:
        copy.wait()


def collect(plan, pieces, scale, whole, base):
    taps, depth, channels = pieces[0].shape
    count = len(pieces)
    operands = list(pieces)
    specs = [VMEM] * count
    aliases = {}
    if base is not None:
        operands.append(base)
        specs.append(ANY)
        aliases = {count: 0}
    return call(
        functools.partial(collect_kernel, scale, plan),
        1 << 20,
        count << 19,
        in_specs=specs,
        out_specs=ANY,
        out_shape=pltpu.HBM(whole, F32),
        input_output_aliases=aliases,
        scratch_shapes=[
            pltpu.VMEM((count, taps, depth, channels), F32),
            pltpu.SemaphoreType.DMA((count,)),
        ],
    )(*operands)


def backward_kernel(codes, pos, act, grad, cross, link, weights, act_out, out, inner, edge, made, sems):
    slots, side, _, channels = grad.shape
    store = pltpu.make_async_copy(act, act_out, sems.at[slots])
    store.start()
    for tile in range(slots):
        put_inner(inner, grad, codes, tile, tile)
        put_edges(
            edge, lambda slot, row: grad[slot, row].astype(F32),
            side, slots, cross, link, codes, tile,
        )
    stores = [store]
    for tile in range(slots):
        total = None
        for row_step in range(3):
            rows = rows_for(inner, edge, tile, row_step).reshape(side * side, 3 * channels)
            for col_step in range(3):
                tap = 3 * (2 - row_step) + 2 - col_step
                part = lax.dot_general(
                    rows[:, col_step * channels : (col_step + 1) * channels],
                    weights[tap * channels : (tap + 1) * channels],
                    (((1,), (1,)), ((), ())),
                    preferred_element_type=F32,
                )
                total = part if total is None else total + part
        gate = jnp.where(pos[tile] >= 0, 1.0, 0.0)
        made[tile] = (total * gate).astype(BF16).reshape(side, side, channels)
        store = pltpu.make_async_copy(made.at[tile], out.at[tile], sems.at[tile])
        store.start()
        stores.append(store)
    for store in stores:
        store.wait()


def backward(codes, pos, act, grad, cross, link, weights):
    slots, side, _, channels = grad.shape
    return call(
        backward_kernel,
        18 * slots * side * side * channels * channels,
        4 << 20,
        in_specs=[SMEM, SMEM] + [VMEM] * 5,
        out_specs=[ANY, ANY],
        out_shape=[pltpu.HBM(grad.shape, BF16)] * 2,
        scratch_shapes=[
            pltpu.VMEM((slots, side, side, 3 * channels), BF16),
            pltpu.VMEM((slots, 2, side, 3 * channels), BF16),
            pltpu.VMEM(grad.shape, BF16),
            pltpu.SemaphoreType.DMA((slots + 1,)),
        ],
    )(codes, pos, act, grad, cross, link, weights)


def edge_swaps(to_core, to_link):
    count = lax.axis_size("tile")
    ends = [(s, s + 1) for s in range(1, count - 1, 2)]
    link = lax.ppermute(to_link, "tile", ends + [(t, s) for s, t in ends])
    return swap(to_core, 1), link


def swap(value, bit):
    count = lax.axis_size("tile")
    return lax.ppermute(value, "tile", [(source, source ^ bit) for source in range(count)])


def sum_high(total, high):
    shape = total.shape
    index = lax.axis_index("tile")
    for bit in high[:-1]:
        flat = total.reshape(2, -1, shape[-1])
        upper = (index & bit) != 0
        arrived = swap(jnp.where(upper, flat[0], flat[1]).astype(BF16), bit)
        total = jnp.where(upper, flat[1], flat[0]) + arrived.astype(F32)
    mine = total.astype(BF16)
    other = swap(mine, high[-1])
    total = (mine.astype(F32) + other.astype(F32)).astype(BF16)
    for bit in reversed(high[:-1]):
        upper = (index & bit) != 0
        other = swap(total, bit)
        total = jnp.concatenate(
            [jnp.where(upper, other, total), jnp.where(upper, total, other)], axis=0
        )
    return total.reshape(shape)


def step(features, weights, grad_out, tile_pos, neighbours):
    slots, side, _, channels = features.shape
    devices = lax.axis_size("tile")
    flat = weights.reshape(9 * channels, channels)
    inner, flat, grads, to_core, to_link = load(neighbours, features, flat, grad_out)
    cross, link = edge_swaps(to_core, to_link)
    partial = product(inner, flat)
    activation, grad, edge, to_core, to_link = forward(
        neighbours, tile_pos, partial, inner, cross, link, flat, grads
    )
    send = kernel_grad(True, inner, edge, grad, BF16)
    recv = swap(send, 1)
    keep = kernel_grad(False, inner, edge, grad, F32)
    own, *sends = spread(keep, recv)
    got = [swap(sends[k], 2 * (k + 1)) for k in (2, 0, 1)]
    total = own + got[0].astype(F32) + got[1].astype(F32) + got[2].astype(F32)
    piece = sum_high(total, [8 << k for k in range(devices.bit_length() - 4)])
    scale = 1.0 / math.sqrt(slots * devices * side * side)
    whole = weights.shape
    pieces = [piece] + [swap(piece, 2 * k) for k in (1, 2, 3)]
    its = [swap(piece, 1)]
    its += [swap(item, 1) for item in pieces[1:3]]
    its.append(swap(pieces[3], 1))
    weight_grad = collect(((0, 0), (1, 0)), [pieces[0], its[0]], scale, whole, None)
    weight_grad = collect(
        ((0, 1), (0, 2), (0, 3), (1, 1), (1, 2)),
        pieces[1:] + its[1:3], scale, whole, weight_grad,
    )
    weight_grad = collect(((1, 3),), its[3:], scale, whole, weight_grad)
    cross, link = edge_swaps(to_core, to_link)
    activation, input_grad = backward(
        neighbours, tile_pos, activation, grad, cross, link,
        weights.reshape(9 * channels, channels),
    )
    return (activation, weight_grad, input_grad)


def solution(mesh):
    in_specs = (
        P(("groups", "tile"), None, None, None),
        P(),
        P(("groups", "tile"), None, None, None),
        P(("groups", "tile")),
        P(("groups", "tile"), None),
    )
    out_specs = (
        P(("groups", "tile"), None, None, None),
        P("groups", None, None),
        P(("groups", "tile"), None, None, None),
    )
    return jax.shard_map(step, mesh=mesh, in_specs=in_specs, out_specs=out_specs, check_vma=False)
```

```python
import functools
import math

import jax
import jax.numpy as jnp
from jax import lax
from jax.experimental import pallas as pl
from jax.experimental.pallas import tpu as pltpu
from jax.sharding import PartitionSpec as P


ROOT_HALF = 0.7071067811865476
INV_ROOT_TAU = 0.3989422804014327
F32 = jnp.float32
BF16 = jnp.bfloat16
VMEM = pl.BlockSpec(memory_space=pltpu.VMEM)
SMEM = pl.BlockSpec(memory_space=pltpu.SMEM)
ANY = pl.BlockSpec(memory_space=pl.ANY)
LIMIT = 16 << 20


def held(shape, dtype):
    return pltpu.VMEM(shape, dtype)


def far(value):
    return pltpu.with_memory_space_constraint(value, pltpu.HBM)


def call(kernel, flops, moved, **options):
    return pl.pallas_call(
        kernel,
        compiler_params=pltpu.CompilerParams(vmem_limit_bytes=LIMIT),
        cost_estimate=pl.CostEstimate(flops=flops, bytes_accessed=moved, transcendentals=0),
        **options,
    )


def place():
    index = lax.axis_index("tile").astype(jnp.int32)
    return lax.rem(index, 2), lax.rem(lax.div(index, 2), 4)


def put_edges(out, own_row, side, slots, cross, link, codes, tile):
    core = place()[0]

    def named(code, row, begin, of_other_core):
        own = own_row(jnp.clip(code - slots, 0, slots - 1), row)
        away = jnp.clip(code - begin, 0, slots - 1)
        away = jnp.where(of_other_core, cross[away].astype(F32), link[away].astype(F32))
        inside = (code >= slots) & (code < 2 * slots)
        return jnp.where(inside, own, jnp.where(code >= 0, away, 0.0))

    top = [named(codes[tile, j], side - 1, 0, core == 1) for j in (0, 4, 5)]
    put_columns(out, (tile, 0), *top)
    bottom = [named(codes[tile, j], 0, 2 * slots, core == 0) for j in (1, 6, 7)]
    put_columns(out, (tile, 1), *bottom)


def put_sends(to_core, to_link, tile, first, last):
    even = place()[0] == 0
    to_core[tile] = jnp.where(even, last.astype(F32), first.astype(F32)).astype(BF16)
    to_link[tile] = jnp.where(even, first.astype(F32), last.astype(F32)).astype(BF16)


def put_columns(out, at, center, left, right):
    axis = center.ndim - 2
    side, channels = center.shape[-2:]
    cell = lax.broadcasted_iota(jnp.int32, center.shape, axis)
    shifted = pltpu.roll(jnp.where(cell == side - 1, left, center), 1, axis)
    out[at + (Ellipsis, slice(0, channels))] = shifted.astype(BF16)
    out[at + (Ellipsis, slice(channels, 2 * channels))] = center.astype(BF16)
    shifted = pltpu.roll(jnp.where(cell == 0, right, center), side - 1, axis)
    out[at + (Ellipsis, slice(2 * channels, 3 * channels))] = shifted.astype(BF16)


def put_inner(out, maps, codes, tile, at):
    slots = maps.shape[0]

    def neighbour(code):
        return jnp.where(code >= 0, maps[jnp.clip(code - slots, 0, slots - 1)].astype(F32), 0.0)

    put_columns(
        out, (at,), maps[tile].astype(F32), neighbour(codes[tile, 2]), neighbour(codes[tile, 3])
    )


def rows_for(inner, edge, tile, step):
    side = inner.shape[1]
    if step == 1:
        return inner[tile]
    if step == 0:
        return jnp.concatenate([edge[tile, 0][None], inner[tile, : side - 1]], axis=0)
    return jnp.concatenate([inner[tile, 1:], edge[tile, 1][None]], axis=0)


def inner_product(inner, weights, tile):
    side, _, wide = inner.shape[1:]
    channels = wide // 3
    total = jnp.dot(
        inner[tile].reshape(side * side, wide),
        weights[wide : 2 * wide],
        preferred_element_type=F32,
    )
    blank = jnp.zeros((side, channels), F32)
    short = (side - 1) * side
    upper = jnp.dot(
        inner[tile, : side - 1].reshape(short, wide), weights[:wide], preferred_element_type=F32
    )
    lower = jnp.dot(
        inner[tile, 1:].reshape(short, wide), weights[2 * wide :], preferred_element_type=F32
    )
    total += jnp.concatenate([blank, upper], axis=0)
    total += jnp.concatenate([lower, blank], axis=0)
    return total.reshape(side, side, channels)


def load_kernel(
    codes, maps, weights, grads, inner, weights_out, grads_out, to_core, to_link, tiles, sems
):
    loads = [
        pltpu.make_async_copy(source, target, sems.at[k])
        for k, (source, target) in enumerate(
            [(maps, tiles), (weights, weights_out), (grads, grads_out)]
        )
    ]
    for load in loads:
        load.start()
    loads[0].wait()
    slots, side = maps.shape[:2]
    for tile in range(slots):
        put_sends(to_core, to_link, tile, tiles[tile, 0], tiles[tile, side - 1])
        put_inner(inner, tiles, codes, tile, tile)
    loads[1].wait()
    loads[2].wait()


def load(codes, maps, weights, grads):
    slots, side, _, channels = maps.shape
    rims = (slots, side, channels)
    return call(
        load_kernel,
        1 << 20,
        6 << 20,
        in_specs=[SMEM, ANY, ANY, ANY],
        out_specs=[VMEM] * 5,
        out_shape=[
            held((slots, side, side, 3 * channels), BF16),
            held(weights.shape, BF16),
            held(grads.shape, BF16),
            held(rims, BF16),
            held(rims, BF16),
        ],
        scratch_shapes=[pltpu.VMEM(maps.shape, BF16), pltpu.SemaphoreType.DMA((3,))],
    )(far(codes), far(maps), far(weights), far(grads))


def finished(value, outer, pos):
    gate = jnp.where(pos >= 0, 1.0, 0.0)
    cumulative = 0.5 * (1.0 + lax.erf(value * ROOT_HALF))
    density = jnp.exp(-0.5 * value * value) * INV_ROOT_TAU
    slope = cumulative + value * density
    made = outer.astype(F32) * slope * gate
    return (value * cumulative * gate).astype(BF16), made.astype(BF16)


def product_kernel(early, pos, inner, weights, grads, partial, act, grad, pos_held, sem):
    slots, side = inner.shape[:2]
    arrival = pltpu.make_async_copy(pos, pos_held, sem)
    arrival.start()
    rows = slice(1, side - 1)
    partial[0] = inner_product(inner, weights, 0)
    arrival.wait()
    for tile in range(slots):
        if tile + 1 < slots:
            partial[tile + 1] = inner_product(inner, weights, tile + 1)
        if tile < early:
            act[tile, rows], grad[tile, rows] = finished(
                partial[tile, rows], grads[tile, rows], pos_held[tile]
            )


def product(early, pos, inner, weights, grads):
    slots, side, _, wide = inner.shape
    return call(
        functools.partial(product_kernel, early),
        2 * slots * side * side * wide * wide,
        6 << 20,
        in_specs=[ANY] + [VMEM] * 3,
        out_specs=[VMEM] * 3,
        out_shape=[
            held((slots, side, side, wide // 3), F32),
            held(grads.shape, BF16),
            held(grads.shape, BF16),
        ],
        scratch_shapes=[pltpu.SMEM(pos.shape, jnp.int32), pltpu.SemaphoreType.DMA],
    )(far(pos), inner, weights, grads)


def forward_kernel(
    early, codes, pos, partial, inner, cross, link, weights, grads, act_in, grad_in,
    act, grad, edge, to_core, to_link, codes_held, pos_held, sems,
):
    slots, side, _, channels = partial.shape
    wide = 3 * channels
    loads = [
        pltpu.make_async_copy(codes, codes_held, sems.at[0]),
        pltpu.make_async_copy(pos, pos_held, sems.at[1]),
    ]
    for item in loads:
        item.start()
    loads[1].wait()
    rows = slice(1, side - 1)
    for tile in range(early, slots):
        act[tile, rows], grad[tile, rows] = finished(
            partial[tile, rows], grads[tile, rows], pos_held[tile]
        )
    loads[0].wait()
    center = slice(channels, 2 * channels)
    for tile in range(slots):
        put_edges(
            edge, lambda slot, row: inner[slot, row, :, center].astype(F32),
            side, slots, cross, link, codes_held, tile,
        )
    ends = []
    for end, row, part in ((0, 0, 0), (1, side - 1, 2)):
        added = jnp.dot(
            edge[:, end].reshape(slots * side, wide),
            weights[part * wide : (part + 1) * wide],
            preferred_element_type=F32,
        ).reshape(slots, side, channels)
        made = []
        for tile in range(slots):
            value, outer = finished(
                partial[tile, row] + added[tile], grads[tile, row], pos_held[tile]
            )
            act[tile, row] = value
            grad[tile, row] = outer
            made.append(outer)
        ends.append(made)
    for tile in range(slots):
        put_sends(to_core, to_link, tile, ends[0][tile], ends[1][tile])


def forward(early, codes, pos, partial, inner, cross, link, weights, grads, act, grad):
    slots, side, _, channels = partial.shape
    wide = 3 * channels
    return call(
        functools.partial(forward_kernel, early),
        4 * slots * side * wide * channels,
        8 << 20,
        in_specs=[ANY, ANY] + [VMEM] * 8,
        out_specs=[VMEM] * 5,
        out_shape=[
            held(partial.shape, BF16),
            held(partial.shape, BF16),
            held((slots, 2, side, wide), BF16),
            held(cross.shape, BF16),
            held(cross.shape, BF16),
        ],
        input_output_aliases={8: 0, 9: 1},
        scratch_shapes=[
            pltpu.SMEM(codes.shape, jnp.int32),
            pltpu.SMEM(pos.shape, jnp.int32),
            pltpu.SemaphoreType.DMA((2,)),
        ],
    )(far(codes), far(pos), partial, inner, cross, link, weights, grads, act, grad)


def kernel_grad_kernel(other, inner, edge, grad, out):
    slots, side, _, channels = grad.shape
    lanes = channels // 2
    outer = grad[...].reshape(slots * side * side, channels)
    core = place()[0]
    half = 1 - core if other else core
    for row_step in range(3):
        for col_step in range(3):
            start = pl.multiple_of(col_step * channels + half * lanes, lanes)
            part = pl.ds(start, lanes)
            if row_step == 1:
                rows = inner[:, :, :, part]
            elif row_step == 0:
                rows = jnp.concatenate([edge[:, :1, :, part], inner[:, : side - 1, :, part]], axis=1)
            else:
                rows = jnp.concatenate([inner[:, 1:, :, part], edge[:, 1:, :, part]], axis=1)
            made = lax.dot_general(
                rows.reshape(slots * side * side, lanes),
                outer,
                (((0,), (0,)), ((), ())),
                preferred_element_type=F32,
            )
            out[:, 3 * row_step + col_step] = made.reshape(4, lanes // 4, channels).astype(out.dtype)


def kernel_grad(other, inner, edge, grad, dtype):
    slots, side, _, channels = grad.shape
    return call(
        functools.partial(kernel_grad_kernel, other),
        9 * slots * side * side * channels * channels,
        6 << 20,
        in_specs=[VMEM, VMEM, VMEM],
        out_specs=VMEM,
        out_shape=held((4, 9, channels // 8, channels), dtype),
    )(inner, edge, grad)


def spread_kernel(keep, recv, own, *sends):
    quad = place()[1]
    own[...] = keep[quad] + recv[quad].astype(F32)
    for k, send in enumerate(sends):
        other = quad ^ (k + 1)
        send[...] = (keep[other] + recv[other].astype(F32)).astype(BF16)


def spread(keep, recv):
    piece = keep.shape[1:]
    return call(
        spread_kernel,
        1 << 20,
        3 << 20,
        in_specs=[VMEM, VMEM],
        out_specs=[VMEM] * 4,
        out_shape=[held(piece, F32)] + [held(piece, BF16)] * 3,
    )(keep, recv)


def collect_kernel(scale, plan, *refs):
    count = len(plan)
    core, quad = place()
    pieces, out = refs[:count], refs[-3]
    rows, sem = refs[-2], refs[-1]
    depth = pieces[0].shape[-2]
    copies = []
    for k, piece in enumerate(pieces):
        rows[k] = piece[...].astype(F32) * scale
        half = 1 - core if plan[k][0] else core
        slot = half * 4 + (quad ^ plan[k][1])
        start = pl.multiple_of(slot * depth, depth)
        copy = pltpu.make_async_copy(rows.at[k], out.at[:, pl.ds(start, depth), :], sem.at[k])
        copy.start()
        copies.append(copy)
    for copy in copies:
        copy.wait()


def collect(plan, pieces, scale, whole, base):
    taps, depth, channels = pieces[0].shape
    count = len(pieces)
    operands = list(pieces)
    specs = [VMEM] * count
    aliases = {}
    if base is not None:
        operands.append(base)
        specs.append(ANY)
        aliases = {count: 0}
    return call(
        functools.partial(collect_kernel, scale, plan),
        1 << 20,
        count << 19,
        in_specs=specs,
        out_specs=ANY,
        out_shape=pltpu.HBM(whole, F32),
        input_output_aliases=aliases,
        scratch_shapes=[
            pltpu.VMEM((count, taps, depth, channels), F32),
            pltpu.SemaphoreType.DMA((count,)),
        ],
    )(*operands)


def backward_kernel(codes, pos, act, grad, cross, link, weights, act_out, out, inner, edge, made, sems):
    slots, side, _, channels = grad.shape
    store = pltpu.make_async_copy(act, act_out, sems.at[slots])
    store.start()
    for tile in range(slots):
        put_inner(inner, grad, codes, tile, tile)
        put_edges(
            edge, lambda slot, row: grad[slot, row].astype(F32),
            side, slots, cross, link, codes, tile,
        )
    stores = [store]
    for tile in range(slots):
        total = None
        for row_step in range(3):
            rows = rows_for(inner, edge, tile, row_step).reshape(side * side, 3 * channels)
            for col_step in range(3):
                tap = 3 * (2 - row_step) + 2 - col_step
                part = lax.dot_general(
                    rows[:, col_step * channels : (col_step + 1) * channels],
                    weights[tap * channels : (tap + 1) * channels],
                    (((1,), (1,)), ((), ())),
                    preferred_element_type=F32,
                )
                total = part if total is None else total + part
        gate = jnp.where(pos[tile] >= 0, 1.0, 0.0)
        made[tile] = (total * gate).astype(BF16).reshape(side, side, channels)
        store = pltpu.make_async_copy(made.at[tile], out.at[tile], sems.at[tile])
        store.start()
        stores.append(store)
    for store in stores:
        store.wait()


def backward(codes, pos, act, grad, cross, link, weights):
    slots, side, _, channels = grad.shape
    return call(
        backward_kernel,
        18 * slots * side * side * channels * channels,
        4 << 20,
        in_specs=[SMEM, SMEM] + [VMEM] * 5,
        out_specs=[ANY, ANY],
        out_shape=[pltpu.HBM(grad.shape, BF16)] * 2,
        scratch_shapes=[
            pltpu.VMEM((slots, side, side, 3 * channels), BF16),
            pltpu.VMEM((slots, 2, side, 3 * channels), BF16),
            pltpu.VMEM(grad.shape, BF16),
            pltpu.SemaphoreType.DMA((slots + 1,)),
        ],
    )(codes, pos, act, grad, cross, link, weights)


def edge_swaps(to_core, to_link):
    count = lax.axis_size("tile")
    ends = [(s, s + 1) for s in range(1, count - 1, 2)]
    link = lax.ppermute(to_link, "tile", ends + [(t, s) for s, t in ends])
    return swap(to_core, 1), link


def swap(value, bit):
    count = lax.axis_size("tile")
    return lax.ppermute(value, "tile", [(source, source ^ bit) for source in range(count)])


def quad_swaps(values):
    got = []
    for k, value in enumerate(values):
        got.append(swap(value, 2 * (k + 1)))
    return got


def sum_high(total, high):
    shape = total.shape
    index = lax.axis_index("tile")
    for bit in high[:-1]:
        flat = total.reshape(2, -1, shape[-1])
        upper = (index & bit) != 0
        arrived = swap(jnp.where(upper, flat[0], flat[1]).astype(BF16), bit)
        total = jnp.where(upper, flat[1], flat[0]) + arrived.astype(F32)
    mine = total.astype(BF16)
    other = swap(mine, high[-1])
    total = (mine.astype(F32) + other.astype(F32)).astype(BF16)
    for bit in reversed(high[:-1]):
        upper = (index & bit) != 0
        other = swap(total, bit)
        total = jnp.concatenate(
            [jnp.where(upper, other, total), jnp.where(upper, total, other)], axis=0
        )
    return total.reshape(shape)


def step(features, weights, grad_out, tile_pos, neighbours):
    slots, side, _, channels = features.shape
    devices = lax.axis_size("tile")
    flat = weights.reshape(9 * channels, channels)
    early = slots
    inner, flat, grads, to_core, to_link = load(neighbours, features, flat, grad_out)
    cross, link = edge_swaps(to_core, to_link)
    partial, activation, grad = product(early, tile_pos, inner, flat, grads)
    activation, grad, edge, to_core, to_link = forward(
        early, neighbours, tile_pos, partial, inner, cross, link, flat, grads, activation, grad
    )
    send = kernel_grad(True, inner, edge, grad, BF16)
    recv = swap(send, 1)
    keep = kernel_grad(False, inner, edge, grad, F32)
    own, *sends = spread(keep, recv)
    got = quad_swaps(sends)
    total = own + got[0].astype(F32) + got[1].astype(F32) + got[2].astype(F32)
    piece = sum_high(total, [8 << k for k in range(devices.bit_length() - 4)])
    scale = 1.0 / math.sqrt(slots * devices * side * side)
    whole = weights.shape
    pieces = [piece] + quad_swaps([piece] * 3)
    its = [swap(piece, 1)]
    its += [swap(item, 1) for item in pieces[1:3]]
    its.append(swap(pieces[3], 1))
    weight_grad = collect(((0, 0), (1, 0)), [pieces[0], its[0]], scale, whole, None)
    weight_grad = collect(
        ((0, 1), (0, 2), (0, 3), (1, 1), (1, 2)),
        pieces[1:] + its[1:3], scale, whole, weight_grad,
    )
    weight_grad = collect(((1, 3),), its[3:], scale, whole, weight_grad)
    cross, link = edge_swaps(to_core, to_link)
    activation, input_grad = backward(
        neighbours, tile_pos, activation, grad, cross, link,
        weights.reshape(9 * channels, channels),
    )
    return (activation, weight_grad, input_grad)


def solution(mesh):
    in_specs = (
        P(("groups", "tile"), None, None, None),
        P(),
        P(("groups", "tile"), None, None, None),
        P(("groups", "tile")),
        P(("groups", "tile"), None),
    )
    out_specs = (
        P(("groups", "tile"), None, None, None),
        P("groups", None, None),
        P(("groups", "tile"), None, None, None),
    )
    return jax.shard_map(step, mesh=mesh, in_specs=in_specs, out_specs=out_specs, check_vma=False)
```

```python
import functools
import math

import jax
import jax.numpy as jnp
from jax import lax
from jax.experimental import pallas as pl
from jax.experimental.pallas import tpu as pltpu
from jax.sharding import PartitionSpec as P


ROOT_HALF = 0.7071067811865476
INV_ROOT_TAU = 0.3989422804014327
F32 = jnp.float32
BF16 = jnp.bfloat16
VMEM = pl.BlockSpec(memory_space=pltpu.VMEM)
SMEM = pl.BlockSpec(memory_space=pltpu.SMEM)
ANY = pl.BlockSpec(memory_space=pl.ANY)
LIMIT = 16 << 20


def held(shape, dtype):
    return pltpu.VMEM(shape, dtype)


def far(value):
    return pltpu.with_memory_space_constraint(value, pltpu.HBM)


def call(kernel, flops, moved, **options):
    return pl.pallas_call(
        kernel,
        compiler_params=pltpu.CompilerParams(vmem_limit_bytes=LIMIT),
        cost_estimate=pl.CostEstimate(flops=flops, bytes_accessed=moved, transcendentals=0),
        **options,
    )


def place():
    index = lax.axis_index("tile").astype(jnp.int32)
    return lax.rem(index, 2), lax.rem(lax.div(index, 2), 4)


def reach(core, k):
    return jnp.where(core == 0, k, 3 - k) if k in (1, 2) else k


def put_edges(out, own_row, side, slots, cross, link, codes, tile):
    core = place()[0]

    def named(code, row, begin, of_other_core):
        own = own_row(jnp.clip(code - slots, 0, slots - 1), row)
        away = jnp.clip(code - begin, 0, slots - 1)
        away = jnp.where(of_other_core, cross[away].astype(F32), link[away].astype(F32))
        inside = (code >= slots) & (code < 2 * slots)
        return jnp.where(inside, own, jnp.where(code >= 0, away, 0.0))

    top = [named(codes[tile, j], side - 1, 0, core == 1) for j in (0, 4, 5)]
    put_columns(out, (tile, 0), *top)
    bottom = [named(codes[tile, j], 0, 2 * slots, core == 0) for j in (1, 6, 7)]
    put_columns(out, (tile, 1), *bottom)


def put_sends(to_core, to_link, tile, first, last):
    even = place()[0] == 0
    to_core[tile] = jnp.where(even, last.astype(F32), first.astype(F32)).astype(BF16)
    to_link[tile] = jnp.where(even, first.astype(F32), last.astype(F32)).astype(BF16)


def put_columns(out, at, center, left, right):
    axis = center.ndim - 2
    side, channels = center.shape[-2:]
    cell = lax.broadcasted_iota(jnp.int32, center.shape, axis)
    shifted = pltpu.roll(jnp.where(cell == side - 1, left, center), 1, axis)
    out[at + (Ellipsis, slice(0, channels))] = shifted.astype(BF16)
    out[at + (Ellipsis, slice(channels, 2 * channels))] = center.astype(BF16)
    shifted = pltpu.roll(jnp.where(cell == 0, right, center), side - 1, axis)
    out[at + (Ellipsis, slice(2 * channels, 3 * channels))] = shifted.astype(BF16)


def put_inner(out, maps, codes, tile, at):
    slots = maps.shape[0]

    def neighbour(code):
        return jnp.where(code >= 0, maps[jnp.clip(code - slots, 0, slots - 1)].astype(F32), 0.0)

    put_columns(
        out, (at,), maps[tile].astype(F32), neighbour(codes[tile, 2]), neighbour(codes[tile, 3])
    )


def rows_for(inner, edge, tile, step):
    side = inner.shape[1]
    if step == 1:
        return inner[tile]
    if step == 0:
        return jnp.concatenate([edge[tile, 0][None], inner[tile, : side - 1]], axis=0)
    return jnp.concatenate([inner[tile, 1:], edge[tile, 1][None]], axis=0)


def inner_product(inner, weights, tile):
    side, _, wide = inner.shape[1:]
    channels = wide // 3
    total = jnp.dot(
        inner[tile].reshape(side * side, wide),
        weights[wide : 2 * wide],
        preferred_element_type=F32,
    )
    blank = jnp.zeros((side, channels), F32)
    short = (side - 1) * side
    upper = jnp.dot(
        inner[tile, : side - 1].reshape(short, wide), weights[:wide], preferred_element_type=F32
    )
    lower = jnp.dot(
        inner[tile, 1:].reshape(short, wide), weights[2 * wide :], preferred_element_type=F32
    )
    total += jnp.concatenate([blank, upper], axis=0)
    total += jnp.concatenate([lower, blank], axis=0)
    return total.reshape(side, side, channels)


def load_kernel(
    codes, maps, weights, grads, inner, weights_out, grads_out, to_core, to_link, tiles, sems
):
    loads = [
        pltpu.make_async_copy(source, target, sems.at[k])
        for k, (source, target) in enumerate(
            [(maps, tiles), (weights, weights_out), (grads, grads_out)]
        )
    ]
    for load in loads:
        load.start()
    loads[0].wait()
    slots, side = maps.shape[:2]
    for tile in range(slots):
        put_sends(to_core, to_link, tile, tiles[tile, 0], tiles[tile, side - 1])
        put_inner(inner, tiles, codes, tile, tile)
    loads[1].wait()
    loads[2].wait()


def load(codes, maps, weights, grads):
    slots, side, _, channels = maps.shape
    rims = (slots, side, channels)
    return call(
        load_kernel,
        1 << 20,
        6 << 20,
        in_specs=[SMEM, ANY, ANY, ANY],
        out_specs=[VMEM] * 5,
        out_shape=[
            held((slots, side, side, 3 * channels), BF16),
            held(weights.shape, BF16),
            held(grads.shape, BF16),
            held(rims, BF16),
            held(rims, BF16),
        ],
        scratch_shapes=[pltpu.VMEM(maps.shape, BF16), pltpu.SemaphoreType.DMA((3,))],
    )(far(codes), far(maps), far(weights), far(grads))


def finished(value, outer, pos):
    gate = jnp.where(pos >= 0, 1.0, 0.0)
    cumulative = 0.5 * (1.0 + lax.erf(value * ROOT_HALF))
    density = jnp.exp(-0.5 * value * value) * INV_ROOT_TAU
    slope = cumulative + value * density
    made = outer.astype(F32) * slope * gate
    return (value * cumulative * gate).astype(BF16), made.astype(BF16)


def product_kernel(early, pos, inner, weights, grads, partial, act, grad, pos_held, sem):
    slots, side = inner.shape[:2]
    arrival = pltpu.make_async_copy(pos, pos_held, sem)
    arrival.start()
    rows = slice(1, side - 1)
    partial[0] = inner_product(inner, weights, 0)
    arrival.wait()
    for tile in range(slots):
        if tile + 1 < slots:
            partial[tile + 1] = inner_product(inner, weights, tile + 1)
        if tile < early:
            act[tile, rows], grad[tile, rows] = finished(
                partial[tile, rows], grads[tile, rows], pos_held[tile]
            )


def product(early, pos, inner, weights, grads):
    slots, side, _, wide = inner.shape
    return call(
        functools.partial(product_kernel, early),
        2 * slots * side * side * wide * wide,
        6 << 20,
        in_specs=[ANY] + [VMEM] * 3,
        out_specs=[VMEM] * 3,
        out_shape=[
            held((slots, side, side, wide // 3), F32),
            held(grads.shape, BF16),
            held(grads.shape, BF16),
        ],
        scratch_shapes=[pltpu.SMEM(pos.shape, jnp.int32), pltpu.SemaphoreType.DMA],
    )(far(pos), inner, weights, grads)


def forward_kernel(
    early, codes, pos, partial, inner, cross, link, weights, grads, act_in, grad_in,
    act, grad, edge, to_core, to_link, codes_held, pos_held, sems,
):
    slots, side, _, channels = partial.shape
    wide = 3 * channels
    loads = [
        pltpu.make_async_copy(codes, codes_held, sems.at[0]),
        pltpu.make_async_copy(pos, pos_held, sems.at[1]),
    ]
    for item in loads:
        item.start()
    loads[1].wait()
    rows = slice(1, side - 1)
    for tile in range(early, slots):
        act[tile, rows], grad[tile, rows] = finished(
            partial[tile, rows], grads[tile, rows], pos_held[tile]
        )
    loads[0].wait()
    center = slice(channels, 2 * channels)
    for tile in range(slots):
        put_edges(
            edge, lambda slot, row: inner[slot, row, :, center].astype(F32),
            side, slots, cross, link, codes_held, tile,
        )
    ends = []
    for end, row, part in ((0, 0, 0), (1, side - 1, 2)):
        added = jnp.dot(
            edge[:, end].reshape(slots * side, wide),
            weights[part * wide : (part + 1) * wide],
            preferred_element_type=F32,
        ).reshape(slots, side, channels)
        made = []
        for tile in range(slots):
            value, outer = finished(
                partial[tile, row] + added[tile], grads[tile, row], pos_held[tile]
            )
            act[tile, row] = value
            grad[tile, row] = outer
            made.append(outer)
        ends.append(made)
    for tile in range(slots):
        put_sends(to_core, to_link, tile, ends[0][tile], ends[1][tile])


def forward(early, codes, pos, partial, inner, cross, link, weights, grads, act, grad):
    slots, side, _, channels = partial.shape
    wide = 3 * channels
    return call(
        functools.partial(forward_kernel, early),
        4 * slots * side * wide * channels,
        8 << 20,
        in_specs=[ANY, ANY] + [VMEM] * 8,
        out_specs=[VMEM] * 5,
        out_shape=[
            held(partial.shape, BF16),
            held(partial.shape, BF16),
            held((slots, 2, side, wide), BF16),
            held(cross.shape, BF16),
            held(cross.shape, BF16),
        ],
        input_output_aliases={8: 0, 9: 1},
        scratch_shapes=[
            pltpu.SMEM(codes.shape, jnp.int32),
            pltpu.SMEM(pos.shape, jnp.int32),
            pltpu.SemaphoreType.DMA((2,)),
        ],
    )(far(codes), far(pos), partial, inner, cross, link, weights, grads, act, grad)


def kernel_grad_kernel(other, inner, edge, grad, out):
    slots, side, _, channels = grad.shape
    lanes = channels // 2
    outer = grad[...].reshape(slots * side * side, channels)
    core = place()[0]
    half = 1 - core if other else core
    for row_step in range(3):
        for col_step in range(3):
            start = pl.multiple_of(col_step * channels + half * lanes, lanes)
            part = pl.ds(start, lanes)
            if row_step == 1:
                rows = inner[:, :, :, part]
            elif row_step == 0:
                rows = jnp.concatenate([edge[:, :1, :, part], inner[:, : side - 1, :, part]], axis=1)
            else:
                rows = jnp.concatenate([inner[:, 1:, :, part], edge[:, 1:, :, part]], axis=1)
            made = lax.dot_general(
                rows.reshape(slots * side * side, lanes),
                outer,
                (((0,), (0,)), ((), ())),
                preferred_element_type=F32,
            )
            out[:, 3 * row_step + col_step] = made.reshape(4, lanes // 4, channels).astype(out.dtype)


def kernel_grad(other, inner, edge, grad, dtype):
    slots, side, _, channels = grad.shape
    return call(
        functools.partial(kernel_grad_kernel, other),
        9 * slots * side * side * channels * channels,
        6 << 20,
        in_specs=[VMEM, VMEM, VMEM],
        out_specs=VMEM,
        out_shape=held((4, 9, channels // 8, channels), dtype),
    )(inner, edge, grad)


def spread_kernel(keep, recv, own, *sends):
    core, quad = place()
    own[...] = keep[quad] + recv[quad].astype(F32)
    for k, send in enumerate(sends):
        other = quad ^ reach(core, k + 1)
        send[...] = (keep[other] + recv[other].astype(F32)).astype(BF16)


def spread(keep, recv):
    piece = keep.shape[1:]
    return call(
        spread_kernel,
        1 << 20,
        3 << 20,
        in_specs=[VMEM, VMEM],
        out_specs=[VMEM] * 4,
        out_shape=[held(piece, F32)] + [held(piece, BF16)] * 3,
    )(keep, recv)


def collect_kernel(scale, plan, *refs):
    count = len(plan)
    core, quad = place()
    pieces, out = refs[:count], refs[-3]
    rows, sem = refs[-2], refs[-1]
    depth = pieces[0].shape[-2]
    copies = []
    for k, piece in enumerate(pieces):
        rows[k] = piece[...].astype(F32) * scale
        half = 1 - core if plan[k][0] else core
        slot = half * 4 + (quad ^ reach(half, plan[k][1]))
        start = pl.multiple_of(slot * depth, depth)
        copy = pltpu.make_async_copy(rows.at[k], out.at[:, pl.ds(start, depth), :], sem.at[k])
        copy.start()
        copies.append(copy)
    for copy in copies:
        copy.wait()


def collect(plan, pieces, scale, whole, base):
    taps, depth, channels = pieces[0].shape
    count = len(pieces)
    operands = list(pieces)
    specs = [VMEM] * count
    aliases = {}
    if base is not None:
        operands.append(base)
        specs.append(ANY)
        aliases = {count: 0}
    return call(
        functools.partial(collect_kernel, scale, plan),
        1 << 20,
        count << 19,
        in_specs=specs,
        out_specs=ANY,
        out_shape=pltpu.HBM(whole, F32),
        input_output_aliases=aliases,
        scratch_shapes=[
            pltpu.VMEM((count, taps, depth, channels), F32),
            pltpu.SemaphoreType.DMA((count,)),
        ],
    )(*operands)


def backward_kernel(codes, pos, act, grad, cross, link, weights, act_out, out, inner, edge, made, sems):
    slots, side, _, channels = grad.shape
    store = pltpu.make_async_copy(act, act_out, sems.at[slots])
    store.start()
    for tile in range(slots):
        put_inner(inner, grad, codes, tile, tile)
        put_edges(
            edge, lambda slot, row: grad[slot, row].astype(F32),
            side, slots, cross, link, codes, tile,
        )
    stores = [store]
    for tile in range(slots):
        total = None
        for row_step in range(3):
            rows = rows_for(inner, edge, tile, row_step).reshape(side * side, 3 * channels)
            for col_step in range(3):
                tap = 3 * (2 - row_step) + 2 - col_step
                part = lax.dot_general(
                    rows[:, col_step * channels : (col_step + 1) * channels],
                    weights[tap * channels : (tap + 1) * channels],
                    (((1,), (1,)), ((), ())),
                    preferred_element_type=F32,
                )
                total = part if total is None else total + part
        gate = jnp.where(pos[tile] >= 0, 1.0, 0.0)
        made[tile] = (total * gate).astype(BF16).reshape(side, side, channels)
        store = pltpu.make_async_copy(made.at[tile], out.at[tile], sems.at[tile])
        store.start()
        stores.append(store)
    for store in stores:
        store.wait()


def backward(codes, pos, act, grad, cross, link, weights):
    slots, side, _, channels = grad.shape
    return call(
        backward_kernel,
        18 * slots * side * side * channels * channels,
        4 << 20,
        in_specs=[SMEM, SMEM] + [VMEM] * 5,
        out_specs=[ANY, ANY],
        out_shape=[pltpu.HBM(grad.shape, BF16)] * 2,
        scratch_shapes=[
            pltpu.VMEM((slots, side, side, 3 * channels), BF16),
            pltpu.VMEM((slots, 2, side, 3 * channels), BF16),
            pltpu.VMEM(grad.shape, BF16),
            pltpu.SemaphoreType.DMA((slots + 1,)),
        ],
    )(codes, pos, act, grad, cross, link, weights)


def edge_swaps(to_core, to_link):
    groups, count = lax.axis_size("groups"), lax.axis_size("tile")
    pairs = []
    for group in range(groups):
        other = group ^ 1 if groups % 2 == 0 else group
        for s in range(count):
            if s in (0, count - 1):
                t = s if other != group else count - 1 - s
                pairs.append((group * count + s, other * count + t))
            else:
                pairs.append((group * count + s, group * count + (s + 1 if s & 1 else s - 1)))
    link = lax.ppermute(to_link, ("groups", "tile"), pairs)
    return swap(to_core, 1), link


def swap(value, bit):
    count = lax.axis_size("tile")
    return lax.ppermute(value, "tile", [(source, source ^ bit) for source in range(count)])


def quad_swaps(values):
    count = lax.axis_size("tile")
    got = []
    for k, value in enumerate(values):
        even, odd = 2 * (k + 1), 2 * (2 - k if k < 2 else 3)
        pairs = [(s, s ^ (odd if s & 1 else even)) for s in range(count)]
        got.append(lax.ppermute(value, "tile", pairs))
    return got


def sum_high(total, high):
    shape = total.shape
    index = lax.axis_index("tile")
    for bit in high[:-1]:
        flat = total.reshape(2, -1, shape[-1])
        upper = (index & bit) != 0
        arrived = swap(jnp.where(upper, flat[0], flat[1]).astype(BF16), bit)
        total = jnp.where(upper, flat[1], flat[0]) + arrived.astype(F32)
    mine = total.astype(BF16)
    other = swap(mine, high[-1])
    total = (mine.astype(F32) + other.astype(F32)).astype(BF16)
    for bit in reversed(high[:-1]):
        upper = (index & bit) != 0
        other = swap(total, bit)
        total = jnp.concatenate(
            [jnp.where(upper, other, total), jnp.where(upper, total, other)], axis=0
        )
    return total.reshape(shape)


def step(features, weights, grad_out, tile_pos, neighbours):
    slots, side, _, channels = features.shape
    devices = lax.axis_size("tile")
    flat = weights.reshape(9 * channels, channels)
    early = slots
    inner, flat, grads, to_core, to_link = load(neighbours, features, flat, grad_out)
    cross, link = edge_swaps(to_core, to_link)
    partial, activation, grad = product(early, tile_pos, inner, flat, grads)
    activation, grad, edge, to_core, to_link = forward(
        early, neighbours, tile_pos, partial, inner, cross, link, flat, grads, activation, grad
    )
    send = kernel_grad(True, inner, edge, grad, BF16)
    recv = swap(send, 1)
    keep = kernel_grad(False, inner, edge, grad, F32)
    own, *sends = spread(keep, recv)
    got = quad_swaps(sends)
    total = own + got[0].astype(F32) + got[1].astype(F32) + got[2].astype(F32)
    piece = sum_high(total, [8 << k for k in range(devices.bit_length() - 4)])
    scale = 1.0 / math.sqrt(slots * devices * side * side)
    whole = weights.shape
    pieces = [piece] + quad_swaps([piece] * 3)
    its = [swap(piece, 1)]
    its += [swap(item, 1) for item in pieces[1:3]]
    its.append(swap(pieces[3], 1))
    weight_grad = collect(((0, 0), (1, 0)), [pieces[0], its[0]], scale, whole, None)
    weight_grad = collect(
        ((0, 1), (0, 2), (0, 3), (1, 1), (1, 2)),
        pieces[1:] + its[1:3], scale, whole, weight_grad,
    )
    weight_grad = collect(((1, 3),), its[3:], scale, whole, weight_grad)
    cross, link = edge_swaps(to_core, to_link)
    activation, input_grad = backward(
        neighbours, tile_pos, activation, grad, cross, link,
        weights.reshape(9 * channels, channels),
    )
    return (activation, weight_grad, input_grad)


def solution(mesh):
    in_specs = (
        P(("groups", "tile"), None, None, None),
        P(),
        P(("groups", "tile"), None, None, None),
        P(("groups", "tile")),
        P(("groups", "tile"), None),
    )
    out_specs = (
        P(("groups", "tile"), None, None, None),
        P("groups", None, None),
        P(("groups", "tile"), None, None, None),
    )
    return jax.shard_map(step, mesh=mesh, in_specs=in_specs, out_specs=out_specs, check_vma=False)
```

```python
import functools
import math

import jax
import jax.numpy as jnp
from jax import lax
from jax.experimental import pallas as pl
from jax.experimental.pallas import tpu as pltpu
from jax.sharding import PartitionSpec as P


ROOT_HALF = 0.7071067811865476
INV_ROOT_TAU = 0.3989422804014327
F32 = jnp.float32
BF16 = jnp.bfloat16
VMEM = pl.BlockSpec(memory_space=pltpu.VMEM)
SMEM = pl.BlockSpec(memory_space=pltpu.SMEM)
ANY = pl.BlockSpec(memory_space=pl.ANY)
LIMIT = 16 << 20


def held(shape, dtype):
    return pltpu.VMEM(shape, dtype)


def far(value):
    return pltpu.with_memory_space_constraint(value, pltpu.HBM)


def call(kernel, flops, moved, **options):
    return pl.pallas_call(
        kernel,
        compiler_params=pltpu.CompilerParams(vmem_limit_bytes=LIMIT),
        cost_estimate=pl.CostEstimate(flops=flops, bytes_accessed=moved, transcendentals=0),
        **options,
    )


def place():
    index = lax.axis_index("tile").astype(jnp.int32)
    return lax.rem(index, 2), lax.rem(lax.div(index, 2), 4)


def reach(core, k):
    return jnp.where(core == 0, k, 3 - k) if k in (1, 2) else k


def put_edges(out, own_row, side, slots, cross, link, codes, tile):
    core = place()[0]

    def named(code, row, begin, of_other_core):
        own = own_row(jnp.clip(code - slots, 0, slots - 1), row)
        away = jnp.clip(code - begin, 0, slots - 1)
        away = jnp.where(of_other_core, cross[away].astype(F32), link[away].astype(F32))
        inside = (code >= slots) & (code < 2 * slots)
        return jnp.where(inside, own, jnp.where(code >= 0, away, 0.0))

    top = [named(codes[tile, j], side - 1, 0, core == 1) for j in (0, 4, 5)]
    put_columns(out, (tile, 0), *top)
    bottom = [named(codes[tile, j], 0, 2 * slots, core == 0) for j in (1, 6, 7)]
    put_columns(out, (tile, 1), *bottom)


def put_sends(to_core, to_link, tile, first, last):
    even = place()[0] == 0
    to_core[tile] = jnp.where(even, last.astype(F32), first.astype(F32)).astype(BF16)
    to_link[tile] = jnp.where(even, first.astype(F32), last.astype(F32)).astype(BF16)


def put_columns(out, at, center, left, right):
    axis = center.ndim - 2
    side, channels = center.shape[-2:]
    cell = lax.broadcasted_iota(jnp.int32, center.shape, axis)
    shifted = pltpu.roll(jnp.where(cell == side - 1, left, center), 1, axis)
    out[at + (Ellipsis, slice(0, channels))] = shifted.astype(BF16)
    out[at + (Ellipsis, slice(channels, 2 * channels))] = center.astype(BF16)
    shifted = pltpu.roll(jnp.where(cell == 0, right, center), side - 1, axis)
    out[at + (Ellipsis, slice(2 * channels, 3 * channels))] = shifted.astype(BF16)


def put_inner(out, maps, codes, tile, at):
    slots = maps.shape[0]

    def neighbour(code):
        return jnp.where(code >= 0, maps[jnp.clip(code - slots, 0, slots - 1)].astype(F32), 0.0)

    put_columns(
        out, (at,), maps[tile].astype(F32), neighbour(codes[tile, 2]), neighbour(codes[tile, 3])
    )


def rows_for(inner, edge, tile, step):
    side = inner.shape[1]
    if step == 1:
        return inner[tile]
    if step == 0:
        return jnp.concatenate([edge[tile, 0][None], inner[tile, : side - 1]], axis=0)
    return jnp.concatenate([inner[tile, 1:], edge[tile, 1][None]], axis=0)


def inner_product(inner, weights, tile):
    side, _, wide = inner.shape[1:]
    channels = wide // 3
    total = jnp.dot(
        inner[tile].reshape(side * side, wide),
        weights[wide : 2 * wide],
        preferred_element_type=F32,
    )
    blank = jnp.zeros((side, channels), F32)
    short = (side - 1) * side
    upper = jnp.dot(
        inner[tile, : side - 1].reshape(short, wide), weights[:wide], preferred_element_type=F32
    )
    lower = jnp.dot(
        inner[tile, 1:].reshape(short, wide), weights[2 * wide :], preferred_element_type=F32
    )
    total += jnp.concatenate([blank, upper], axis=0)
    total += jnp.concatenate([lower, blank], axis=0)
    return total.reshape(side, side, channels)


def load_kernel(
    codes, maps, weights, grads, inner, weights_out, grads_out, to_core, to_link, tiles, sems
):
    loads = [
        pltpu.make_async_copy(source, target, sems.at[k])
        for k, (source, target) in enumerate(
            [(maps, tiles), (weights, weights_out), (grads, grads_out)]
        )
    ]
    for load in loads:
        load.start()
    loads[0].wait()
    slots, side = maps.shape[:2]
    for tile in range(slots):
        put_sends(to_core, to_link, tile, tiles[tile, 0], tiles[tile, side - 1])
        put_inner(inner, tiles, codes, tile, tile)
    loads[1].wait()
    loads[2].wait()


def load(codes, maps, weights, grads):
    slots, side, _, channels = maps.shape
    rims = (slots, side, channels)
    return call(
        load_kernel,
        1 << 20,
        6 << 20,
        in_specs=[SMEM, ANY, ANY, ANY],
        out_specs=[VMEM] * 5,
        out_shape=[
            held((slots, side, side, 3 * channels), BF16),
            held(weights.shape, BF16),
            held(grads.shape, BF16),
            held(rims, BF16),
            held(rims, BF16),
        ],
        scratch_shapes=[pltpu.VMEM(maps.shape, BF16), pltpu.SemaphoreType.DMA((3,))],
    )(far(codes), far(maps), far(weights), far(grads))


def finished(value, outer, pos):
    gate = jnp.where(pos >= 0, 1.0, 0.0)
    cumulative = 0.5 * (1.0 + lax.erf(value * ROOT_HALF))
    density = jnp.exp(-0.5 * value * value) * INV_ROOT_TAU
    slope = cumulative + value * density
    made = outer.astype(F32) * slope * gate
    return (value * cumulative * gate).astype(BF16), made.astype(BF16)


def product_kernel(early, pos, inner, weights, grads, partial, act, grad, pos_held, sem):
    slots, side = inner.shape[:2]
    arrival = pltpu.make_async_copy(pos, pos_held, sem)
    arrival.start()
    rows = slice(1, side - 1)
    partial[0] = inner_product(inner, weights, 0)
    arrival.wait()
    for tile in range(slots):
        if tile + 1 < slots:
            partial[tile + 1] = inner_product(inner, weights, tile + 1)
        if tile < early:
            act[tile, rows], grad[tile, rows] = finished(
                partial[tile, rows], grads[tile, rows], pos_held[tile]
            )


def product(early, pos, inner, weights, grads):
    slots, side, _, wide = inner.shape
    return call(
        functools.partial(product_kernel, early),
        2 * slots * side * side * wide * wide,
        6 << 20,
        in_specs=[ANY] + [VMEM] * 3,
        out_specs=[VMEM] * 3,
        out_shape=[
            held((slots, side, side, wide // 3), F32),
            held(grads.shape, BF16),
            held(grads.shape, BF16),
        ],
        scratch_shapes=[pltpu.SMEM(pos.shape, jnp.int32), pltpu.SemaphoreType.DMA],
    )(far(pos), inner, weights, grads)


def forward_kernel(
    early, codes, pos, partial, inner, cross, link, weights, grads, act_in, grad_in,
    act, grad, edge, to_core, to_link, codes_held, pos_held, sems,
):
    slots, side, _, channels = partial.shape
    wide = 3 * channels
    loads = [
        pltpu.make_async_copy(codes, codes_held, sems.at[0]),
        pltpu.make_async_copy(pos, pos_held, sems.at[1]),
    ]
    for item in loads:
        item.start()
    loads[1].wait()
    rows = slice(1, side - 1)
    for tile in range(early, slots):
        act[tile, rows], grad[tile, rows] = finished(
            partial[tile, rows], grads[tile, rows], pos_held[tile]
        )
    loads[0].wait()
    center = slice(channels, 2 * channels)
    for tile in range(slots):
        put_edges(
            edge, lambda slot, row: inner[slot, row, :, center].astype(F32),
            side, slots, cross, link, codes_held, tile,
        )
    ends = []
    for end, row, part in ((0, 0, 0), (1, side - 1, 2)):
        added = jnp.dot(
            edge[:, end].reshape(slots * side, wide),
            weights[part * wide : (part + 1) * wide],
            preferred_element_type=F32,
        ).reshape(slots, side, channels)
        made = []
        for tile in range(slots):
            value, outer = finished(
                partial[tile, row] + added[tile], grads[tile, row], pos_held[tile]
            )
            act[tile, row] = value
            grad[tile, row] = outer
            made.append(outer)
        ends.append(made)
    for tile in range(slots):
        put_sends(to_core, to_link, tile, ends[0][tile], ends[1][tile])


def forward(early, codes, pos, partial, inner, cross, link, weights, grads, act, grad):
    slots, side, _, channels = partial.shape
    wide = 3 * channels
    return call(
        functools.partial(forward_kernel, early),
        4 * slots * side * wide * channels,
        8 << 20,
        in_specs=[ANY, ANY] + [VMEM] * 8,
        out_specs=[VMEM] * 5,
        out_shape=[
            held(partial.shape, BF16),
            held(partial.shape, BF16),
            held((slots, 2, side, wide), BF16),
            held(cross.shape, BF16),
            held(cross.shape, BF16),
        ],
        input_output_aliases={8: 0, 9: 1},
        scratch_shapes=[
            pltpu.SMEM(codes.shape, jnp.int32),
            pltpu.SMEM(pos.shape, jnp.int32),
            pltpu.SemaphoreType.DMA((2,)),
        ],
    )(far(codes), far(pos), partial, inner, cross, link, weights, grads, act, grad)


def kernel_grad_kernel(other, inner, edge, grad, out):
    slots, side, _, channels = grad.shape
    lanes = channels // 2
    outer = grad[...].reshape(slots * side * side, channels)
    core = place()[0]
    half = 1 - core if other else core
    for row_step in range(3):
        for col_step in range(3):
            start = pl.multiple_of(col_step * channels + half * lanes, lanes)
            part = pl.ds(start, lanes)
            if row_step == 1:
                rows = inner[:, :, :, part]
            elif row_step == 0:
                rows = jnp.concatenate([edge[:, :1, :, part], inner[:, : side - 1, :, part]], axis=1)
            else:
                rows = jnp.concatenate([inner[:, 1:, :, part], edge[:, 1:, :, part]], axis=1)
            made = lax.dot_general(
                rows.reshape(slots * side * side, lanes),
                outer,
                (((0,), (0,)), ((), ())),
                preferred_element_type=F32,
            )
            out[:, 3 * row_step + col_step] = made.reshape(4, lanes // 4, channels).astype(out.dtype)


def kernel_grad(other, inner, edge, grad, dtype):
    slots, side, _, channels = grad.shape
    return call(
        functools.partial(kernel_grad_kernel, other),
        9 * slots * side * side * channels * channels,
        6 << 20,
        in_specs=[VMEM, VMEM, VMEM],
        out_specs=VMEM,
        out_shape=held((4, 9, channels // 8, channels), dtype),
    )(inner, edge, grad)


def spread_kernel(keep, recv, own, *sends):
    core, quad = place()
    own[...] = keep[quad] + recv[quad].astype(F32)
    for k, send in enumerate(sends):
        other = quad ^ reach(core, k + 1)
        send[...] = (keep[other] + recv[other].astype(F32)).astype(BF16)


def spread(keep, recv):
    piece = keep.shape[1:]
    return call(
        spread_kernel,
        1 << 20,
        3 << 20,
        in_specs=[VMEM, VMEM],
        out_specs=[VMEM] * 4,
        out_shape=[held(piece, F32)] + [held(piece, BF16)] * 3,
    )(keep, recv)


def collect_kernel(scale, plan, *refs):
    count = len(plan)
    core, quad = place()
    pieces, out = refs[:count], refs[-3]
    rows, sem = refs[-2], refs[-1]
    depth = pieces[0].shape[-2]
    copies = []
    for k, piece in enumerate(pieces):
        rows[k] = piece[...].astype(F32) * scale
        half = 1 - core if plan[k][0] else core
        slot = half * 4 + (quad ^ reach(half, plan[k][1]))
        start = pl.multiple_of(slot * depth, depth)
        copy = pltpu.make_async_copy(rows.at[k], out.at[:, pl.ds(start, depth), :], sem.at[k])
        copy.start()
        copies.append(copy)
    for copy in copies:
        copy.wait()


def collect(plan, pieces, scale, whole, base):
    taps, depth, channels = pieces[0].shape
    count = len(pieces)
    operands = list(pieces)
    specs = [VMEM] * count
    aliases = {}
    if base is not None:
        operands.append(base)
        specs.append(ANY)
        aliases = {count: 0}
    return call(
        functools.partial(collect_kernel, scale, plan),
        1 << 20,
        count << 19,
        in_specs=specs,
        out_specs=ANY,
        out_shape=pltpu.HBM(whole, F32),
        input_output_aliases=aliases,
        scratch_shapes=[
            pltpu.VMEM((count, taps, depth, channels), F32),
            pltpu.SemaphoreType.DMA((count,)),
        ],
    )(*operands)


def backward_kernel(codes, pos, act, grad, cross, link, weights, act_out, out, inner, edge, made, sems):
    slots, side, _, channels = grad.shape
    store = pltpu.make_async_copy(act, act_out, sems.at[slots])
    store.start()
    for tile in range(slots):
        put_inner(inner, grad, codes, tile, tile)
        put_edges(
            edge, lambda slot, row: grad[slot, row].astype(F32),
            side, slots, cross, link, codes, tile,
        )
    stores = [store]
    for tile in range(slots):
        total = None
        for row_step in range(3):
            rows = rows_for(inner, edge, tile, row_step).reshape(side * side, 3 * channels)
            for col_step in range(3):
                tap = 3 * (2 - row_step) + 2 - col_step
                part = lax.dot_general(
                    rows[:, col_step * channels : (col_step + 1) * channels],
                    weights[tap * channels : (tap + 1) * channels],
                    (((1,), (1,)), ((), ())),
                    preferred_element_type=F32,
                )
                total = part if total is None else total + part
        gate = jnp.where(pos[tile] >= 0, 1.0, 0.0)
        made[tile] = (total * gate).astype(BF16).reshape(side, side, channels)
        store = pltpu.make_async_copy(made.at[tile], out.at[tile], sems.at[tile])
        store.start()
        stores.append(store)
    for store in stores:
        store.wait()


def backward(codes, pos, act, grad, cross, link, weights):
    slots, side, _, channels = grad.shape
    return call(
        backward_kernel,
        18 * slots * side * side * channels * channels,
        4 << 20,
        in_specs=[SMEM, SMEM] + [VMEM] * 5,
        out_specs=[ANY, ANY],
        out_shape=[pltpu.HBM(grad.shape, BF16)] * 2,
        scratch_shapes=[
            pltpu.VMEM((slots, side, side, 3 * channels), BF16),
            pltpu.VMEM((slots, 2, side, 3 * channels), BF16),
            pltpu.VMEM(grad.shape, BF16),
            pltpu.SemaphoreType.DMA((slots + 1,)),
        ],
    )(codes, pos, act, grad, cross, link, weights)


def edge_swaps(to_core, to_link):
    groups, count = lax.axis_size("groups"), lax.axis_size("tile")
    pairs = []
    for group in range(groups):
        other = group ^ 1 if groups % 2 == 0 else group
        for s in range(count):
            if s in (0, count - 1):
                t = s if other != group else count - 1 - s
                pairs.append((group * count + s, other * count + t))
            else:
                pairs.append((group * count + s, group * count + (s + 1 if s & 1 else s - 1)))
    link = lax.ppermute(to_link, ("groups", "tile"), pairs)
    return swap(to_core, 1), link


def swap(value, bit):
    count = lax.axis_size("tile")
    return lax.ppermute(value, "tile", [(source, source ^ bit) for source in range(count)])


def quad_swaps(values):
    count = lax.axis_size("tile")
    got = []
    for k, value in enumerate(values):
        even, odd = 2 * (k + 1), 2 * (2 - k if k < 2 else 3)
        pairs = [(s, s ^ (odd if s & 1 else even)) for s in range(count)]
        got.append(lax.ppermute(value, "tile", pairs))
    return got


def sum_high(total, high):
    shape = total.shape
    index = lax.axis_index("tile")
    for bit in high[:-1]:
        flat = total.reshape(2, -1, shape[-1])
        upper = (index & bit) != 0
        arrived = swap(jnp.where(upper, flat[0], flat[1]).astype(BF16), bit)
        total = jnp.where(upper, flat[1], flat[0]) + arrived.astype(F32)
    mine = total.astype(BF16)
    other = swap(mine, high[-1])
    total = (mine.astype(F32) + other.astype(F32)).astype(BF16)
    for bit in reversed(high[:-1]):
        upper = (index & bit) != 0
        other = swap(total, bit)
        total = jnp.concatenate(
            [jnp.where(upper, other, total), jnp.where(upper, total, other)], axis=0
        )
    return total.reshape(shape)


def step(features, weights, grad_out, tile_pos, neighbours):
    slots, side, _, channels = features.shape
    devices = lax.axis_size("tile")
    flat = weights.reshape(9 * channels, channels)
    early = slots
    inner, flat, grads, to_core, to_link = load(neighbours, features, flat, grad_out)
    cross, link = edge_swaps(to_core, to_link)
    partial, activation, grad = product(early, tile_pos, inner, flat, grads)
    activation, grad, edge, to_core, to_link = forward(
        early, neighbours, tile_pos, partial, inner, cross, link, flat, grads, activation, grad
    )
    send = kernel_grad(True, inner, edge, grad, BF16)
    recv = swap(send, 1)
    keep = kernel_grad(False, inner, edge, grad, F32)
    own, *sends = spread(keep, recv)
    got = quad_swaps(sends)
    total = own + got[0].astype(F32) + got[1].astype(F32) + got[2].astype(F32)
    piece = sum_high(total, [8 << k for k in range(devices.bit_length() - 4)])
    scale = 1.0 / math.sqrt(slots * devices * side * side)
    whole = weights.shape
    pieces = [piece] + quad_swaps([piece] * 3)
    its = [swap(piece, 1)]
    its += [swap(item, 1) for item in pieces[1:3]]
    its.append(swap(pieces[3], 1))
    weight_grad = collect(((0, 0), (1, 0)), [pieces[0], its[0]], scale, whole, None)
    weight_grad = collect(
        ((0, 1), (0, 2), (0, 3)),
        pieces[1:], scale, whole, weight_grad,
    )
    weight_grad = collect(((1, 1), (1, 2), (1, 3)), its[1:], scale, whole, weight_grad)
    cross, link = edge_swaps(to_core, to_link)
    activation, input_grad = backward(
        neighbours, tile_pos, activation, grad, cross, link,
        weights.reshape(9 * channels, channels),
    )
    return (activation, weight_grad, input_grad)


def solution(mesh):
    in_specs = (
        P(("groups", "tile"), None, None, None),
        P(),
        P(("groups", "tile"), None, None, None),
        P(("groups", "tile")),
        P(("groups", "tile"), None),
    )
    out_specs = (
        P(("groups", "tile"), None, None, None),
        P("groups", None, None),
        P(("groups", "tile"), None, None, None),
    )
    return jax.shard_map(step, mesh=mesh, in_specs=in_specs, out_specs=out_specs, check_vma=False)
```

```python
import functools
import math

import jax
import jax.numpy as jnp
from jax import lax
from jax.experimental import pallas as pl
from jax.experimental.pallas import tpu as pltpu
from jax.sharding import PartitionSpec as P


ROOT_HALF = 0.7071067811865476
INV_ROOT_TAU = 0.3989422804014327
F32 = jnp.float32
BF16 = jnp.bfloat16
VMEM = pl.BlockSpec(memory_space=pltpu.VMEM)
SMEM = pl.BlockSpec(memory_space=pltpu.SMEM)
ANY = pl.BlockSpec(memory_space=pl.ANY)
LIMIT = 16 << 20


def held(shape, dtype):
    return pltpu.VMEM(shape, dtype)


def far(value):
    return pltpu.with_memory_space_constraint(value, pltpu.HBM)


def call(kernel, flops, moved, **options):
    return pl.pallas_call(
        kernel,
        compiler_params=pltpu.CompilerParams(vmem_limit_bytes=LIMIT),
        cost_estimate=pl.CostEstimate(flops=flops, bytes_accessed=moved, transcendentals=0),
        **options,
    )


def place():
    index = lax.axis_index("tile").astype(jnp.int32)
    return lax.rem(index, 2), lax.rem(lax.div(index, 2), 4)


def reach(core, k):
    return jnp.where(core == 0, k, 3 - k) if k in (1, 2) else k


def put_edges(out, own_row, side, slots, cross, link, codes, tile):
    core = place()[0]

    def named(code, row, begin, of_other_core):
        own = own_row(jnp.clip(code - slots, 0, slots - 1), row)
        away = jnp.clip(code - begin, 0, slots - 1)
        away = jnp.where(of_other_core, cross[away].astype(F32), link[away].astype(F32))
        inside = (code >= slots) & (code < 2 * slots)
        return jnp.where(inside, own, jnp.where(code >= 0, away, 0.0))

    top = [named(codes[tile, j], side - 1, 0, core == 1) for j in (0, 4, 5)]
    put_columns(out, (tile, 0), *top)
    bottom = [named(codes[tile, j], 0, 2 * slots, core == 0) for j in (1, 6, 7)]
    put_columns(out, (tile, 1), *bottom)


def put_sends(to_core, to_link, tile, first, last):
    even = place()[0] == 0
    to_core[tile] = jnp.where(even, last.astype(F32), first.astype(F32)).astype(BF16)
    to_link[tile] = jnp.where(even, first.astype(F32), last.astype(F32)).astype(BF16)


def put_columns(out, at, center, left, right):
    axis = center.ndim - 2
    side, channels = center.shape[-2:]
    cell = lax.broadcasted_iota(jnp.int32, center.shape, axis)
    shifted = pltpu.roll(jnp.where(cell == side - 1, left, center), 1, axis)
    out[at + (Ellipsis, slice(0, channels))] = shifted.astype(BF16)
    out[at + (Ellipsis, slice(channels, 2 * channels))] = center.astype(BF16)
    shifted = pltpu.roll(jnp.where(cell == 0, right, center), side - 1, axis)
    out[at + (Ellipsis, slice(2 * channels, 3 * channels))] = shifted.astype(BF16)


def put_inner(out, maps, codes, tile, at):
    slots = maps.shape[0]

    def neighbour(code):
        return jnp.where(code >= 0, maps[jnp.clip(code - slots, 0, slots - 1)].astype(F32), 0.0)

    put_columns(
        out, (at,), maps[tile].astype(F32), neighbour(codes[tile, 2]), neighbour(codes[tile, 3])
    )


def rows_for(inner, edge, tile, step):
    side = inner.shape[1]
    if step == 1:
        return inner[tile]
    if step == 0:
        return jnp.concatenate([edge[tile, 0][None], inner[tile, : side - 1]], axis=0)
    return jnp.concatenate([inner[tile, 1:], edge[tile, 1][None]], axis=0)


def inner_product(inner, weights, tile):
    side, _, wide = inner.shape[1:]
    channels = wide // 3
    total = jnp.dot(
        inner[tile].reshape(side * side, wide),
        weights[wide : 2 * wide],
        preferred_element_type=F32,
    )
    blank = jnp.zeros((side, channels), F32)
    short = (side - 1) * side
    upper = jnp.dot(
        inner[tile, : side - 1].reshape(short, wide), weights[:wide], preferred_element_type=F32
    )
    lower = jnp.dot(
        inner[tile, 1:].reshape(short, wide), weights[2 * wide :], preferred_element_type=F32
    )
    total += jnp.concatenate([blank, upper], axis=0)
    total += jnp.concatenate([lower, blank], axis=0)
    return total.reshape(side, side, channels)


def load_kernel(
    codes, maps, weights, grads, inner, weights_out, grads_out, to_core, to_link, tiles, sems
):
    loads = [
        pltpu.make_async_copy(source, target, sems.at[k])
        for k, (source, target) in enumerate(
            [(maps, tiles), (weights, weights_out), (grads, grads_out)]
        )
    ]
    for load in loads:
        load.start()
    loads[0].wait()
    slots, side = maps.shape[:2]
    for tile in range(slots):
        put_sends(to_core, to_link, tile, tiles[tile, 0], tiles[tile, side - 1])
        put_inner(inner, tiles, codes, tile, tile)
    loads[1].wait()
    loads[2].wait()


def load(codes, maps, weights, grads):
    slots, side, _, channels = maps.shape
    rims = (slots, side, channels)
    return call(
        load_kernel,
        1 << 20,
        6 << 20,
        in_specs=[SMEM, ANY, ANY, ANY],
        out_specs=[VMEM] * 5,
        out_shape=[
            held((slots, side, side, 3 * channels), BF16),
            held(weights.shape, BF16),
            held(grads.shape, BF16),
            held(rims, BF16),
            held(rims, BF16),
        ],
        scratch_shapes=[pltpu.VMEM(maps.shape, BF16), pltpu.SemaphoreType.DMA((3,))],
    )(far(codes), far(maps), far(weights), far(grads))


def finished(value, outer, pos):
    gate = jnp.where(pos >= 0, 1.0, 0.0)
    cumulative = 0.5 * (1.0 + lax.erf(value * ROOT_HALF))
    density = jnp.exp(-0.5 * value * value) * INV_ROOT_TAU
    slope = cumulative + value * density
    made = outer.astype(F32) * slope * gate
    return (value * cumulative * gate).astype(BF16), made.astype(BF16)


def product_kernel(early, pos, inner, weights, grads, partial, act, grad, pos_held, sem):
    slots, side = inner.shape[:2]
    arrival = pltpu.make_async_copy(pos, pos_held, sem)
    arrival.start()
    rows = slice(1, side - 1)
    partial[0] = inner_product(inner, weights, 0)
    arrival.wait()
    for tile in range(slots):
        if tile + 1 < slots:
            partial[tile + 1] = inner_product(inner, weights, tile + 1)
        if tile < early:
            act[tile, rows], grad[tile, rows] = finished(
                partial[tile, rows], grads[tile, rows], pos_held[tile]
            )


def product(early, pos, inner, weights, grads):
    slots, side, _, wide = inner.shape
    return call(
        functools.partial(product_kernel, early),
        2 * slots * side * side * wide * wide,
        6 << 20,
        in_specs=[ANY] + [VMEM] * 3,
        out_specs=[VMEM] * 3,
        out_shape=[
            held((slots, side, side, wide // 3), F32),
            held(grads.shape, BF16),
            held(grads.shape, BF16),
        ],
        scratch_shapes=[pltpu.SMEM(pos.shape, jnp.int32), pltpu.SemaphoreType.DMA],
    )(far(pos), inner, weights, grads)


def forward_kernel(
    early, codes, pos, partial, inner, cross, link, weights, grads, act_in, grad_in,
    act, grad, edge, to_core, to_link, codes_held, pos_held, sems,
):
    slots, side, _, channels = partial.shape
    wide = 3 * channels
    loads = [
        pltpu.make_async_copy(codes, codes_held, sems.at[0]),
        pltpu.make_async_copy(pos, pos_held, sems.at[1]),
    ]
    for item in loads:
        item.start()
    loads[1].wait()
    rows = slice(1, side - 1)
    for tile in range(early, slots):
        act[tile, rows], grad[tile, rows] = finished(
            partial[tile, rows], grads[tile, rows], pos_held[tile]
        )
    loads[0].wait()
    center = slice(channels, 2 * channels)
    for tile in range(slots):
        put_edges(
            edge, lambda slot, row: inner[slot, row, :, center].astype(F32),
            side, slots, cross, link, codes_held, tile,
        )
    ends = []
    for end, row, part in ((0, 0, 0), (1, side - 1, 2)):
        added = jnp.dot(
            edge[:, end].reshape(slots * side, wide),
            weights[part * wide : (part + 1) * wide],
            preferred_element_type=F32,
        ).reshape(slots, side, channels)
        made = []
        for tile in range(slots):
            value, outer = finished(
                partial[tile, row] + added[tile], grads[tile, row], pos_held[tile]
            )
            act[tile, row] = value
            grad[tile, row] = outer
            made.append(outer)
        ends.append(made)
    for tile in range(slots):
        put_sends(to_core, to_link, tile, ends[0][tile], ends[1][tile])


def forward(early, codes, pos, partial, inner, cross, link, weights, grads, act, grad):
    slots, side, _, channels = partial.shape
    wide = 3 * channels
    return call(
        functools.partial(forward_kernel, early),
        4 * slots * side * wide * channels,
        8 << 20,
        in_specs=[ANY, ANY] + [VMEM] * 8,
        out_specs=[VMEM] * 5,
        out_shape=[
            held(partial.shape, BF16),
            held(partial.shape, BF16),
            held((slots, 2, side, wide), BF16),
            held(cross.shape, BF16),
            held(cross.shape, BF16),
        ],
        input_output_aliases={8: 0, 9: 1},
        scratch_shapes=[
            pltpu.SMEM(codes.shape, jnp.int32),
            pltpu.SMEM(pos.shape, jnp.int32),
            pltpu.SemaphoreType.DMA((2,)),
        ],
    )(far(codes), far(pos), partial, inner, cross, link, weights, grads, act, grad)


def kernel_grad_kernel(other, inner, edge, grad, out):
    slots, side, _, channels = grad.shape
    lanes = channels // 2
    outer = grad[...].reshape(slots * side * side, channels)
    core = place()[0]
    half = 1 - core if other else core
    for row_step in range(3):
        for col_step in range(3):
            start = pl.multiple_of(col_step * channels + half * lanes, lanes)
            part = pl.ds(start, lanes)
            if row_step == 1:
                rows = inner[:, :, :, part]
            elif row_step == 0:
                rows = jnp.concatenate([edge[:, :1, :, part], inner[:, : side - 1, :, part]], axis=1)
            else:
                rows = jnp.concatenate([inner[:, 1:, :, part], edge[:, 1:, :, part]], axis=1)
            made = lax.dot_general(
                rows.reshape(slots * side * side, lanes),
                outer,
                (((0,), (0,)), ((), ())),
                preferred_element_type=F32,
            )
            out[:, 3 * row_step + col_step] = made.reshape(4, lanes // 4, channels).astype(out.dtype)


def kernel_grad(other, inner, edge, grad, dtype):
    slots, side, _, channels = grad.shape
    return call(
        functools.partial(kernel_grad_kernel, other),
        9 * slots * side * side * channels * channels,
        6 << 20,
        in_specs=[VMEM, VMEM, VMEM],
        out_specs=VMEM,
        out_shape=held((4, 9, channels // 8, channels), dtype),
    )(inner, edge, grad)


def spread_kernel(keep, recv, own, *sends):
    core, quad = place()
    own[...] = keep[quad] + recv[quad].astype(F32)
    for k, send in enumerate(sends):
        other = quad ^ reach(core, k + 1)
        send[...] = (keep[other] + recv[other].astype(F32)).astype(BF16)


def spread(keep, recv):
    piece = keep.shape[1:]
    return call(
        spread_kernel,
        1 << 20,
        3 << 20,
        in_specs=[VMEM, VMEM],
        out_specs=[VMEM] * 4,
        out_shape=[held(piece, F32)] + [held(piece, BF16)] * 3,
    )(keep, recv)


def collect_kernel(scale, plan, *refs):
    count = len(plan)
    core, quad = place()
    pieces, out = refs[:count], refs[-3]
    rows, sem = refs[-2], refs[-1]
    depth = pieces[0].shape[-2]
    copies = []
    for k, piece in enumerate(pieces):
        rows[k] = piece[...].astype(F32) * scale
        half = 1 - core if plan[k][0] else core
        slot = half * 4 + (quad ^ reach(half, plan[k][1]))
        start = pl.multiple_of(slot * depth, depth)
        copy = pltpu.make_async_copy(rows.at[k], out.at[:, pl.ds(start, depth), :], sem.at[k])
        copy.start()
        copies.append(copy)
    for copy in copies:
        copy.wait()


def collect(plan, pieces, scale, whole, base):
    taps, depth, channels = pieces[0].shape
    count = len(pieces)
    operands = list(pieces)
    specs = [VMEM] * count
    aliases = {}
    if base is not None:
        operands.append(base)
        specs.append(ANY)
        aliases = {count: 0}
    return call(
        functools.partial(collect_kernel, scale, plan),
        1 << 20,
        count << 19,
        in_specs=specs,
        out_specs=ANY,
        out_shape=pltpu.HBM(whole, F32),
        input_output_aliases=aliases,
        scratch_shapes=[
            pltpu.VMEM((count, taps, depth, channels), F32),
            pltpu.SemaphoreType.DMA((count,)),
        ],
    )(*operands)


def backward_kernel(codes, pos, act, grad, cross, link, weights, act_out, out, inner, edge, made, sems):
    slots, side, _, channels = grad.shape
    store = pltpu.make_async_copy(act, act_out, sems.at[slots])
    store.start()
    for tile in range(slots):
        put_inner(inner, grad, codes, tile, tile)
        put_edges(
            edge, lambda slot, row: grad[slot, row].astype(F32),
            side, slots, cross, link, codes, tile,
        )
    stores = [store]
    for tile in range(slots):
        total = None
        for row_step in range(3):
            rows = rows_for(inner, edge, tile, row_step).reshape(side * side, 3 * channels)
            for col_step in range(3):
                tap = 3 * (2 - row_step) + 2 - col_step
                part = lax.dot_general(
                    rows[:, col_step * channels : (col_step + 1) * channels],
                    weights[tap * channels : (tap + 1) * channels],
                    (((1,), (1,)), ((), ())),
                    preferred_element_type=F32,
                )
                total = part if total is None else total + part
        gate = jnp.where(pos[tile] >= 0, 1.0, 0.0)
        made[tile] = (total * gate).astype(BF16).reshape(side, side, channels)
        store = pltpu.make_async_copy(made.at[tile], out.at[tile], sems.at[tile])
        store.start()
        stores.append(store)
    for store in stores:
        store.wait()


def backward(codes, pos, act, grad, cross, link, weights):
    slots, side, _, channels = grad.shape
    return call(
        backward_kernel,
        18 * slots * side * side * channels * channels,
        4 << 20,
        in_specs=[SMEM, SMEM] + [VMEM] * 5,
        out_specs=[ANY, ANY],
        out_shape=[pltpu.HBM(grad.shape, BF16)] * 2,
        scratch_shapes=[
            pltpu.VMEM((slots, side, side, 3 * channels), BF16),
            pltpu.VMEM((slots, 2, side, 3 * channels), BF16),
            pltpu.VMEM(grad.shape, BF16),
            pltpu.SemaphoreType.DMA((slots + 1,)),
        ],
    )(codes, pos, act, grad, cross, link, weights)


def edge_swaps(to_core, to_link, ends):
    groups, count = lax.axis_size("groups"), lax.axis_size("tile")
    pairs = []
    for group in range(groups):
        other = group ^ 1 if groups % 2 == 0 else group
        for s in range(count):
            if s in (0, count - 1):
                if not ends:
                    continue
                t = s if other != group else count - 1 - s
                pairs.append((group * count + s, other * count + t))
            else:
                pairs.append((group * count + s, group * count + (s + 1 if s & 1 else s - 1)))
    link = lax.ppermute(to_link, ("groups", "tile"), pairs)
    return swap(to_core, 1), link


def swap(value, bit):
    count = lax.axis_size("tile")
    return lax.ppermute(value, "tile", [(source, source ^ bit) for source in range(count)])


def quad_swaps(values):
    count = lax.axis_size("tile")
    got = []
    for k, value in enumerate(values):
        even, odd = 2 * (k + 1), 2 * (2 - k if k < 2 else 3)
        pairs = [(s, s ^ (odd if s & 1 else even)) for s in range(count)]
        got.append(lax.ppermute(value, "tile", pairs))
    return got


def sum_high(total, high):
    shape = total.shape
    index = lax.axis_index("tile")
    for bit in high[:-1]:
        flat = total.reshape(2, -1, shape[-1])
        upper = (index & bit) != 0
        arrived = swap(jnp.where(upper, flat[0], flat[1]).astype(BF16), bit)
        total = jnp.where(upper, flat[1], flat[0]) + arrived.astype(F32)
    mine = total.astype(BF16)
    other = swap(mine, high[-1])
    total = (mine.astype(F32) + other.astype(F32)).astype(BF16)
    for bit in reversed(high[:-1]):
        upper = (index & bit) != 0
        other = swap(total, bit)
        total = jnp.concatenate(
            [jnp.where(upper, other, total), jnp.where(upper, total, other)], axis=0
        )
    return total.reshape(shape)


def step(features, weights, grad_out, tile_pos, neighbours):
    slots, side, _, channels = features.shape
    devices = lax.axis_size("tile")
    flat = weights.reshape(9 * channels, channels)
    early = slots
    inner, flat, grads, to_core, to_link = load(neighbours, features, flat, grad_out)
    cross, link = edge_swaps(to_core, to_link, True)
    partial, activation, grad = product(early, tile_pos, inner, flat, grads)
    activation, grad, edge, to_core, to_link = forward(
        early, neighbours, tile_pos, partial, inner, cross, link, flat, grads, activation, grad
    )
    send = kernel_grad(True, inner, edge, grad, BF16)
    recv = swap(send, 1)
    keep = kernel_grad(False, inner, edge, grad, F32)
    own, *sends = spread(keep, recv)
    got = quad_swaps(sends)
    total = own + got[0].astype(F32) + got[1].astype(F32) + got[2].astype(F32)
    piece = sum_high(total, [8 << k for k in range(devices.bit_length() - 4)])
    scale = 1.0 / math.sqrt(slots * devices * side * side)
    whole = weights.shape
    pieces = [piece] + quad_swaps([piece] * 3)
    its = [swap(piece, 1)]
    its += [swap(item, 1) for item in pieces[1:3]]
    its.append(swap(pieces[3], 1))
    weight_grad = collect(((0, 0), (1, 0)), [pieces[0], its[0]], scale, whole, None)
    weight_grad = collect(
        ((0, 1), (0, 2), (0, 3), (1, 1), (1, 2)),
        pieces[1:] + its[1:3], scale, whole, weight_grad,
    )
    weight_grad = collect(((1, 3),), its[3:], scale, whole, weight_grad)
    cross, link = edge_swaps(to_core, to_link, False)
    activation, input_grad = backward(
        neighbours, tile_pos, activation, grad, cross, link,
        weights.reshape(9 * channels, channels),
    )
    return (activation, weight_grad, input_grad)


def solution(mesh):
    in_specs = (
        P(("groups", "tile"), None, None, None),
        P(),
        P(("groups", "tile"), None, None, None),
        P(("groups", "tile")),
        P(("groups", "tile"), None),
    )
    out_specs = (
        P(("groups", "tile"), None, None, None),
        P("groups", None, None),
        P(("groups", "tile"), None, None, None),
    )
    return jax.shard_map(step, mesh=mesh, in_specs=in_specs, out_specs=out_specs, check_vma=False)
```
